768 devices in a mesh: sub: 96 (over x, z, core), coarse: 8 (over y).
Axes of the slice: x: 4, y: 8, z: 12, core: 2. Of those that a mesh axis runs over, the one named last changes fastest.
Arguments:
- loads: float32 [96, 8, 16, 16, 128], P('sub', 'coarse'), may hold values from -18 to 18
- mode_x: float32 [96, 8, 16, 16], P('sub', 'coarse'), may hold values from -1 to 2
- mode_y: float32 [96, 8, 16, 16], P('sub', 'coarse'), may hold values from -1 to 2
- mode_z: float32 [96, 8, 128, 128], P('sub', 'coarse'), may hold values from -1 to 2
- eigen: float32 [96, 8, 160], P('sub', 'coarse'), may hold values from 0.1 to 2
- classes: int32 [96, 8, 4, 4, 32], P('sub', 'coarse'), may hold values from 0 to 15
- coefficients: float32 [16], replicated, may hold values from 0.25 to 4
- partner: int32 [96, 8, 4, 2], P('sub', 'coarse'), may hold values from 0 to 95, as said below
- rows: int32 [96, 8, 4, 2048], P('sub', 'coarse'), may hold values from 0 to 32767, as said below
- corner_id: int32 [96, 8, 8], P('sub', 'coarse'), may hold values from 0 to 767, as said below
- corner_row: int32 [96, 8, 8], P('sub', 'coarse'), may hold values from 0 to 32767, as said below
- coarse_inverse: float32 [768, 768], P('coarse'), may hold values from -1 to 3, as said below
Outputs:
- multipliers: float32 [96, 8, 4, 2048], P('sub', 'coarse')
- residual: float32 [96, 8, 4, 2048], P('sub', 'coarse')
The draws below stay inside these ranges and needn't reach their ends.
Inputs may be any that keep to these rules, and one draw needn't show every extreme that they name: partner[i, j, c] differs from (i, j) by one in exactly one index, cyclically; partner[partner[i, j, c], c] = (i, j); the 4 partners of one subdomain are its four cyclic neighbours. `rows`: within one subdomain all 4 x 2048 entries are distinct. `corner_id`: within one subdomain the 8 entries are distinct. `corner_row`: within one subdomain the 8 entries are distinct. `coarse_inverse`: symmetric.
All inputs are finite; a program needn't handle non-finite values.
Results may differ from the reference program's by a relative error of at most 0.0003.
Values sent between devices are 32-bit elements; how exact they have to be, the bound alone decides.
No kernel may reach another device: no remote copies, remote signals or barrier semaphores. Data moves between devices by JAX's collectives and lax.ppermute only.
A program may use at most 32 MiB of HBM per device.

```python
import math
import jax
import jax.numpy as jnp
from jax import lax

GX = 16
GY = 16
GZ = 128
M = 2048
NC = 4
NP = 8
NCLASS = 16
ITERS = 2
NCOARSE = 768
N_SUB = 96
N_COARSE = 8


def local_orders(key, salt, count):
    keys = jax.random.split(jax.random.fold_in(key, salt), N_SUB * N_COARSE)
    return jax.vmap(lambda single: jax.random.permutation(single, GX * GY * GZ)[:count])(keys)


def draw_rows(key, part):
    return local_orders(key, 11, NC * M).reshape(N_SUB, N_COARSE, NC, M).astype(jnp.int32)


def draw_corner_row(key, part):
    return local_orders(key, 23, NP).reshape(N_SUB, N_COARSE, NP).astype(jnp.int32)


def draw_corner_id(key, part):
    keys = jax.random.split(jax.random.fold_in(key, 31), N_SUB * N_COARSE)
    picked = jax.vmap(lambda single: jax.random.permutation(single, NCOARSE)[:NP])(keys)
    return picked.reshape(N_SUB, N_COARSE, NP).astype(jnp.int32)


def draw_partner(key, part):
    roles = jax.random.permutation(jax.random.fold_in(key, 3), 4).astype(jnp.int32)
    first = jnp.broadcast_to(jnp.arange(N_SUB, dtype=jnp.int32)[:, None], (N_SUB, N_COARSE))
    second = jnp.broadcast_to(jnp.arange(N_COARSE, dtype=jnp.int32)[None, :], (N_SUB, N_COARSE))
    sub_even = jnp.where(first % 2 == 0, (first + 1) % N_SUB, (first - 1) % N_SUB)
    sub_odd = jnp.where(first % 2 == 0, (first - 1) % N_SUB, (first + 1) % N_SUB)
    col_even = jnp.where(second % 2 == 0, (second + 1) % N_COARSE, (second - 1) % N_COARSE)
    col_odd = jnp.where(second % 2 == 0, (second - 1) % N_COARSE, (second + 1) % N_COARSE)
    sub_table = jnp.stack([sub_even, sub_odd, first, first], axis=-1)
    col_table = jnp.stack([second, second, col_even, col_odd], axis=-1)
    picked_sub = sub_table[:, :, roles]
    picked_col = col_table[:, :, roles]
    return jnp.stack([picked_sub, picked_col], axis=-1).astype(jnp.int32)


def draw_loads(key, part):
    first = jax.random.fold_in(jax.random.fold_in(key, 5), 0)
    ramp = (3.0 ** (jnp.arange(N_SUB, dtype=jnp.float32) / (N_SUB - 1)))[:, None, None, None, None]
    shape = (N_SUB, N_COARSE, GX, GY, GZ)
    values = jnp.clip(jax.random.normal(first, shape, jnp.float32), -6.0, 6.0)
    return (values * ramp).astype(jnp.float32)


def draw_mode(key, salt, order):
    noise = jax.random.uniform(jax.random.fold_in(key, salt), (N_SUB, N_COARSE, order, order), jnp.float32, -1.0, 1.0)
    amplitude = 0.3
    eye = (jnp.arange(order)[:, None] == jnp.arange(order)[None, :]).astype(jnp.float32)
    return (eye[None, None] + amplitude * (3.0 / order) ** 0.5 * noise).astype(jnp.float32)


def draw_mode_x(key, part):
    return draw_mode(key, 41, GX)


def draw_mode_y(key, part):
    return draw_mode(key, 43, GY)


def draw_mode_z(key, part):
    return draw_mode(key, 47, GZ)


def draw_coarse_inverse(key, part):
    first, second = jax.random.split(jax.random.fold_in(key, 9))
    bound = 0.9 / NCOARSE
    off = jax.random.uniform(first, (NCOARSE, NCOARSE), jnp.float32, -bound, bound)
    off = 0.5 * (off + off.T)
    top = 2.0
    diag = jax.random.uniform(second, (NCOARSE,), jnp.float32, 1.0, top)
    eye = jnp.arange(NCOARSE)[:, None] == jnp.arange(NCOARSE)[None, :]
    return jnp.where(eye, diag[:, None], off).astype(jnp.float32)


def touch_ends(entries, key, low, top_value):
    longest = entries.shape.index(max(entries.shape))
    spots = []
    for shift in (0, 1):
        where = [jax.random.randint(jax.random.fold_in(key, axis), (), 0, length) for axis, length in enumerate(entries.shape)]
        where[longest] = (where[longest] + shift) % entries.shape[longest]
        spots.append(tuple(where))
    return entries.at[spots[0]].set(low).at[spots[1]].set(top_value)


def block_scale(own_key, dims, cuts, low, high):
    def one(axis_at, parts):
        steps = jax.random.uniform(jax.random.fold_in(jax.random.fold_in(own_key, 6), axis_at), (parts,), jnp.float32, low / len(cuts), high / len(cuts))
        return jnp.repeat(jnp.exp(steps), dims[axis_at] // parts).reshape((-1,) + (1,) * (len(dims) - axis_at - 1))

    gain = one(*cuts[0])
    for cut in cuts[1:]:
        gain = gain * one(*cut)
    return gain


def setup_inputs(seed: int = 0) -> dict:
    key_of = jax.random.split(jax.random.key(seed), 13)
    loads = draw_loads(jax.random.fold_in(key_of[12], 71), 0)
    mode_x = draw_mode_x(jax.random.fold_in(key_of[12], 71), 0)
    mode_y = draw_mode_y(jax.random.fold_in(key_of[12], 71), 0)
    mode_z = draw_mode_z(jax.random.fold_in(key_of[12], 71), 0)
    eigen = jnp.clip(jnp.exp(math.log(2.0) - 2.9957323 * jax.random.uniform(key_of[4], (N_SUB, N_COARSE, GX + GY + GZ), jnp.float32) ** block_scale(key_of[4], (N_SUB, N_COARSE, GX + GY + GZ), ((0, 96), (1, 8)), -0.2, 0.2)), 0.1, 2.0)
    classes = touch_ends(jax.random.randint(key_of[5], (N_SUB, N_COARSE, GX // 4, GY // 4, GZ // 4), 0, NCLASS), jax.random.fold_in(key_of[5], 1), 0, NCLASS - 1).astype(jnp.int32)
    coefficients = jnp.clip(jnp.exp(jax.random.uniform(key_of[6], (NCLASS,), jnp.float32, math.log(0.25), math.log(4.0))), 0.25, 4.0)
    partner = draw_partner(jax.random.fold_in(key_of[12], 71), 0)
    rows = draw_rows(jax.random.fold_in(key_of[12], 71), 0)
    corner_id = draw_corner_id(jax.random.fold_in(key_of[12], 71), 0)
    corner_row = draw_corner_row(jax.random.fold_in(key_of[12], 71), 0)
    coarse_inverse = draw_coarse_inverse(jax.random.fold_in(key_of[12], 71), 0)
    return {"loads": loads, "mode_x": mode_x, "mode_y": mode_y, "mode_z": mode_z, "eigen": eigen, "classes": classes, "coefficients": coefficients, "partner": partner, "rows": rows, "corner_id": corner_id, "corner_row": corner_row, "coarse_inverse": coarse_inverse}


def fdm_single(args):
    side_x, side_y, side_z, spectrum, root, field = args
    lam_inv = 1.0 / (spectrum[:GX][:, None, None] + spectrum[GX:GX + GY][None, :, None] + spectrum[GX + GY:][None, None, :])
    values = field * root
    values = jnp.einsum('pa,pyz->ayz', side_x, values, precision=lax.Precision.HIGHEST)
    values = jnp.einsum('pb,xpz->xbz', side_y, values, precision=lax.Precision.HIGHEST)
    values = jnp.einsum('xyp,pc->xyc', values, side_z, precision=lax.Precision.HIGHEST)
    values = values * lam_inv
    values = jnp.einsum('ap,pyz->ayz', side_x, values, precision=lax.Precision.HIGHEST)
    values = jnp.einsum('bp,xpz->xbz', side_y, values, precision=lax.Precision.HIGHEST)
    values = jnp.einsum('xyp,cp->xyc', values, side_z, precision=lax.Precision.HIGHEST)
    return values * root

def reference(loads, mode_x, mode_y, mode_z, eigen, classes, coefficients, partner, rows, corner_id, corner_row, coarse_inverse):
    count = N_SUB * N_COARSE
    nodes = GX * GY * GZ
    coef_elem = coefficients[classes]
    coef_node = jnp.repeat(jnp.repeat(jnp.repeat(coef_elem, 4, axis=2), 4, axis=3), 4, axis=4).reshape(count, GX, GY, GZ)
    root = 1.0 / jnp.sqrt(coef_node)
    side_x = mode_x.reshape(count, GX, GX)
    side_y = mode_y.reshape(count, GY, GY)
    side_z = mode_z.reshape(count, GZ, GZ)
    spectra = eigen.reshape(count, GX + GY + GZ)
    sub_index = jnp.arange(N_SUB, dtype=jnp.int32)[:, None, None]
    col_index = jnp.arange(N_COARSE, dtype=jnp.int32)[None, :, None]
    colour_index = jnp.arange(NC, dtype=jnp.int32)[None, None, :]
    mate_sub = partner[..., 0]
    mate_col = partner[..., 1]
    sign = jnp.where(sub_index * N_COARSE + col_index < mate_sub * N_COARSE + mate_col, 1.0, -1.0).astype(jnp.float32)[..., None]
    rows_flat = rows.reshape(count, NC * M)
    dev_index = jnp.arange(count, dtype=jnp.int32)[:, None]
    crow = corner_row.reshape(count, NP)
    cid = corner_id.reshape(count, NP)

    def partner_of(values):
        return values[mate_sub, mate_col, colour_index]

    def at_rows(field):
        return field[dev_index, rows_flat].reshape(N_SUB, N_COARSE, NC, M)

    def jump(field):
        values = at_rows(field)
        return sign * (values - partner_of(values))

    def solve(field):
        shaped = field.reshape(count, GX, GY, GZ)
        return lax.map(fdm_single, (side_x, side_y, side_z, spectra, root, shaped)).reshape(count, nodes)
    a_rows = coef_node.reshape(count, nodes)[dev_index, rows_flat].reshape(N_SUB, N_COARSE, NC, M)
    a_far = partner_of(a_rows)
    weight = a_rows * a_far / (a_rows + a_far)

    def apply_dual(lam):
        source = jnp.zeros((count, nodes), jnp.float32).at[dev_index, rows_flat].set((sign * lam).reshape(count, NC * M))
        local = solve(source)
        partial_corner = local[dev_index, crow]
        total = jnp.zeros((NCOARSE,), jnp.float32).at[cid.reshape(-1)].add(partial_corner.reshape(-1))
        coarse_sol = jnp.dot(coarse_inverse, total, precision=lax.Precision.HIGHEST)
        extra = jnp.zeros((count, nodes), jnp.float32).at[dev_index, crow].set(coarse_sol[cid])
        return jump(local + solve(extra))
    rhs = jump(solve(loads.reshape(count, nodes)))
    multipliers = jnp.zeros_like(rhs)
    residual = rhs
    precond = weight * residual
    direction = precond
    rz_now = jnp.sum(residual * precond)
    for step in range(ITERS):
        image = apply_dual(direction)
        alpha = rz_now / jnp.sum(direction * image)
        multipliers = multipliers + alpha * direction
        residual = residual - alpha * image
        if step + 1 < ITERS:
            precond = weight * residual
            rz_next = jnp.sum(residual * precond)
            direction = precond + rz_next / rz_now * direction
            rz_now = rz_next
    return (multipliers, residual)
```

```python
import functools

import jax
import jax.numpy as jnp
import numpy as np
from jax import lax
from jax.experimental import pallas as pl
from jax.experimental.pallas import tpu as pltpu
from jax.sharding import Mesh, PartitionSpec as P

F32 = jnp.float32
BF16 = jnp.bfloat16
I32 = jnp.int32

NX, NZ, NCORE, NY = 4, 12, 2, 8
NSUB = NX * NZ * NCORE
PLANE = 256
DEPTH = 128
COLOURS = 4
WIDTH = 2048
CORNERS = 8
TOTAL = 768
CHUNK = 512
NT = (((1,), (1,)), ((), ()))
TN = (((0,), (0,)), ((), ()))


def iota(shape, dim):
    return lax.broadcasted_iota(I32, shape, dim)


def split(x):
    high = x.astype(BF16)
    return high, (x - high.astype(F32)).astype(BF16)


def dot(a, b, dims=None):
    if dims is None:
        return jnp.dot(a, b, preferred_element_type=F32)
    return lax.dot_general(a, b, dims, preferred_element_type=F32)


def dot_full(a, b, dims=(((1,), (0,)), ((), ()))):
    return lax.dot_general(a, b, dims, precision=lax.Precision.HIGHEST, preferred_element_type=F32)


def product(a, b, dims=None):
    (ah, al), (bh, bl) = a, b
    return dot(ah, bh, dims) + (dot(al, bh, dims) + dot(ah, bl, dims))


def position():
    sub = (lax.axis_index("x") * NZ + lax.axis_index("z")) * NCORE + lax.axis_index("core")
    return sub, lax.axis_index("y")


def colour_of_links(partner_ref):
    sub, col = position()
    odd_sub, odd_col = lax.rem(sub, 2), lax.rem(col, 2)
    mates = (
        (sub + 1 - 2 * odd_sub, col),
        (lax.rem(sub + 2 * odd_sub - 1 + NSUB, NSUB), col),
        (sub, col + 1 - 2 * odd_col),
        (sub, lax.rem(col + 2 * odd_col - 1 + NY, NY)),
    )
    links = []
    for mate_sub, mate_col in mates:
        colour = jnp.int32(0)
        for c in range(1, COLOURS):
            hit = (partner_ref[c, 0] == mate_sub) & (partner_ref[c, 1] == mate_col)
            colour = jnp.where(hit, jnp.int32(c), colour)
        links.append(colour)
    return links


def signs(partner_ref):
    sub, col = position()
    me = sub * NY + col
    which = iota((COLOURS, WIDTH), 0)
    result = jnp.full((COLOURS, WIDTH), 1.0, F32)
    for c in range(COLOURS):
        value = jnp.where(me < partner_ref[c, 0] * NY + partner_ref[c, 1], 1.0, -1.0).astype(F32)
        result = jnp.where(which == c, value, result)
    return result


def by_class(classes, table_ref):
    result = jnp.full(classes.shape, table_ref[0], F32)
    for k in range(1, 16):
        result = jnp.where(classes == k, table_ref[k], result)
    return result


def gather(parts, rows_ref, outs):
    stacked = jnp.concatenate([p for group in parts for p in group], axis=0)
    counts = [len(group) for group in parts]

    def step(j, carry):
        here = pl.ds(pl.multiple_of(j * CHUNK, CHUNK), CHUNK)
        for c in range(COLOURS):
            node = rows_ref[c : c + 1, here]
            hot = (iota((PLANE, CHUNK), 0) == (node >> 7)).astype(F32).astype(BF16)
            mask = iota((DEPTH, CHUNK), 0) == (node & 127)
            picked = dot(stacked, hot)
            at = 0
            for out, count in zip(outs, counts):
                total = picked[at * DEPTH : (at + 1) * DEPTH]
                for extra in range(1, count):
                    total = total + picked[(at + extra) * DEPTH : (at + extra + 1) * DEPTH]
                at += count
                out[c : c + 1, here] = jnp.sum(jnp.where(mask, total, 0.0), axis=0, keepdims=True)
        return carry

    lax.fori_loop(0, WIDTH // CHUNK, step, 0)


def scatter(values_ref, rows_ref):
    def step(j, total):
        here = pl.ds(pl.multiple_of(j * CHUNK, CHUNK), CHUNK)
        for c in range(COLOURS):
            node = rows_ref[c : c + 1, here]
            value = values_ref[c : c + 1, here]
            high = value.astype(BF16).astype(F32)
            hot = (iota((PLANE, CHUNK), 0) == (node >> 7)).astype(F32).astype(BF16)
            mask = iota((DEPTH, CHUNK), 0) == (node & 127)
            left = jnp.concatenate(
                [jnp.where(mask, high, 0.0).astype(BF16), jnp.where(mask, value - high, 0.0).astype(BF16)], axis=0
            )
            total = total + dot(left, hot, NT)
        return total

    total = lax.fori_loop(0, WIDTH // CHUNK, step, jnp.zeros((2 * DEPTH, PLANE), F32))
    return total[:DEPTH] + total[DEPTH:]


def forward(field, planes, depths):
    t = product(split(field), (planes[0], planes[1]))
    return product((depths[2], depths[3]), split(t))


def backward(spectrum, planes, depths):
    t = product(split(spectrum), (planes[2], planes[3]))
    return product((depths[0], depths[1]), split(t))


def kernel_start(
    partner_ref, corner_ref, coef_ref, root_ref,
    loads_ref, mode_x_ref, mode_y_ref, mode_z_ref, eigen_ref, classes_ref, rows_ref,
    planes_ref, depths_ref, fields_ref, corners_ref, near_ref, m0_ref, m1_ref, m2_ref, m3_ref,
    cls_ref,
):
    spread_x = (iota((16, PLANE), 0) == (iota((16, PLANE), 1) >> 4)).astype(F32)
    spread_y = (iota((16, PLANE), 0) == (iota((16, PLANE), 1) & 15)).astype(F32)
    wide_x = dot_full(mode_x_ref[...], spread_x)
    wide_y = dot_full(mode_y_ref[...], spread_y)
    tall_x = dot_full(mode_x_ref[...], spread_x, TN)
    tall_y = dot_full(mode_y_ref[...], spread_y, TN)
    for i in range(16):
        here = slice(16 * i, 16 * i + 16)
        high, low = split(wide_x[i : i + 1] * wide_y)
        planes_ref[0, here], planes_ref[1, here] = high, low
        high, low = split(tall_x[i : i + 1] * tall_y)
        planes_ref[2, here], planes_ref[3, here] = high, low
    mode_z = mode_z_ref[...]
    depths_ref[0], depths_ref[1] = split(mode_z)
    depths_ref[2], depths_ref[3] = split(mode_z.T)
    planes = [planes_ref[i] for i in range(4)]
    depths = [depths_ref[i] for i in range(4)]

    line = dot_full(eigen_ref[:, 0:16], spread_x) + dot_full(eigen_ref[:, 16:32], spread_y)
    diagonal = iota((DEPTH, DEPTH), 0) == iota((DEPTH, DEPTH), 1)
    column = jnp.sum(jnp.where(diagonal, eigen_ref[:, 32:160], 0.0), axis=1, keepdims=True)
    lam_inv = 1.0 / (line + column)
    fields_ref[0] = lam_inv

    spread_c = (iota((16, PLANE), 0) == ((iota((16, PLANE), 1) >> 6) * 4 + ((iota((16, PLANE), 1) >> 2) & 3))).astype(BF16)
    spread_d = (iota((DEPTH, 32), 1) == (iota((DEPTH, 32), 0) >> 2)).astype(BF16)
    small = classes_ref[...].astype(F32).astype(BF16)
    deep = dot(spread_d, small, NT).astype(BF16)
    node_class = dot(deep, spread_c)
    class_part = node_class.astype(BF16)
    root = by_class(node_class.astype(I32), root_ref)
    fields_ref[1] = root

    node = jnp.zeros((CORNERS, 1), I32)
    for t in range(CORNERS):
        node = jnp.where(iota((CORNERS, 1), 0) == t, corner_ref[t], node)
    hot_plane = (iota((CORNERS, PLANE), 1) == (node >> 7)).astype(F32)
    hot_depth = (iota((CORNERS, DEPTH), 1) == (node & 127)).astype(F32)
    hot_p, hot_d = hot_plane.astype(BF16), hot_depth.astype(BF16)
    corner_class = jnp.sum(dot(hot_d, class_part) * hot_plane, axis=1, keepdims=True)
    corner_root = by_class(corner_class.astype(I32), root_ref)
    corners_ref[0:8, :] = dot(hot_p, planes[0]) + dot(hot_p, planes[1])
    corners_ref[8:16, 0:DEPTH] = (dot(hot_d, depths[0]) + dot(hot_d, depths[1])) * corner_root
    corners_ref[8:16, DEPTH:] = jnp.zeros((8, PLANE - DEPTH), F32)

    weights = forward(loads_ref[...].T * root, planes, depths) * lam_inv
    high, low = split(backward(weights, planes, depths) * root)
    gather([(high, low), (class_part,)], rows_ref, [near_ref.at[0], cls_ref])
    near_ref[1] = by_class(cls_ref[...].astype(I32), coef_ref)
    for link, message in zip(colour_of_links(partner_ref), (m0_ref, m1_ref, m2_ref, m3_ref)):
        message[0:1, :] = near_ref[0, pl.ds(link, 1), :]
        message[1:2, :] = near_ref[1, pl.ds(link, 1), :]


def reduce_all(x):
    return jnp.sum(jnp.sum(x, axis=1, keepdims=True), axis=0, keepdims=True)


def launch(ids_ref, rows_ref, x_ref, planes, depths, fields_ref, corners_ref, extras, weights_ref, send_ref):
    lam_inv, root = fields_ref[0], fields_ref[1]
    modes = forward(scatter(x_ref, rows_ref) * root, planes, depths)
    weights = modes * lam_inv
    weights_ref[...] = weights
    energy = reduce_all(weights * modes)
    part = dot_full(corners_ref[0:8, :], weights, NT) * corners_ref[8:16, 0:DEPTH]
    part = jnp.sum(part, axis=1, keepdims=True)
    place = iota((8, 128), 0) * 128 + iota((8, 128), 1)
    tile = jnp.zeros((8, 128), F32)
    for t in range(CORNERS):
        tile = tile + jnp.where(place == ids_ref[t], part[t : t + 1, 0:1], 0.0)
    for at, scalar in enumerate([energy] + extras):
        tile = jnp.where(place == TOTAL + at, scalar, tile)
    send_ref[...] = jnp.broadcast_to(tile[None], send_ref.shape)


def receive(partner_ref, messages, far_ref):
    count = messages[0].shape[0]
    for link, message in zip(colour_of_links(partner_ref), messages):
        for i in range(count):
            far_ref[i, pl.ds(link, 1), :] = message[i : i + 1, :]


def kernel_first(
    partner_ref, ids_ref, rows_ref, near_ref, m0_ref, m1_ref, m2_ref, m3_ref,
    planes_ref, depths_ref, fields_ref, corners_ref,
    state_ref, weights_ref, send_ref,
    far_ref, x_ref,
):
    receive(partner_ref, (m0_ref, m1_ref, m2_ref, m3_ref), far_ref)
    sign = signs(partner_ref)
    a, a_far = near_ref[1], far_ref[1]
    rhs = sign * (near_ref[0] - far_ref[0])
    weight = a * a_far / (a + a_far)
    precond = weight * rhs
    state_ref[0] = rhs
    state_ref[1] = weight
    x_ref[...] = sign * precond
    planes = [planes_ref[i] for i in range(4)]
    depths = [depths_ref[i] for i in range(4)]
    launch(
        ids_ref, rows_ref, x_ref, planes, depths, fields_ref, corners_ref, [reduce_all(rhs * precond)],
        weights_ref, send_ref,
    )


def kernel_relay(got_ref, send_ref):
    tile = jnp.sum(got_ref[...], axis=0)
    send_ref[...] = jnp.broadcast_to(tile[None], send_ref.shape)


def kernel_coarse(
    partner_ref, ids_ref, rows_ref, got_ref, inverse_ref, weights_ref,
    planes_ref, depths_ref, fields_ref, corners_ref,
    near_ref, sums_ref, m0_ref, m1_ref, m2_ref, m3_ref,
):
    tile = jnp.sum(got_ref[...], axis=0)
    line = jnp.concatenate([tile[i : i + 1] for i in range(TOTAL // 128)], axis=1)
    high = line.astype(BF16).astype(F32)
    middle = (line - high).astype(BF16).astype(F32)
    low = line - high - middle
    which = iota((8, TOTAL), 0)
    left = jnp.where(which == 0, high, jnp.where(which == 1, middle, jnp.where(which == 2, low, 0.0))).astype(BF16)
    inverse_high, inverse_low = split(inverse_ref[...])
    coarse = jnp.sum(dot(left, inverse_high) + dot(left, inverse_low), axis=0, keepdims=True)
    work = reduce_all(coarse * line)
    scalars = tile[6:7, :]
    sums = jnp.where(iota((8, 128), 1) == 3, work, jnp.broadcast_to(scalars, (8, 128)))
    sums_ref[...] = sums
    ids = jnp.zeros((CORNERS, 1), I32)
    for t in range(CORNERS):
        ids = jnp.where(iota((CORNERS, 1), 0) == t, ids_ref[t], ids)
    own = jnp.sum(jnp.where(iota((CORNERS, TOTAL), 1) == ids, coarse, 0.0), axis=1, keepdims=True)
    lam_inv, root = fields_ref[0], fields_ref[1]
    lifted = dot_full(corners_ref[8:16, 0:DEPTH] * own, corners_ref[0:8, :], TN)
    weights = weights_ref[...] + lam_inv * lifted
    planes = [planes_ref[i] for i in range(4)]
    depths = [depths_ref[i] for i in range(4)]
    high, low = split(backward(weights, planes, depths) * root)
    gather([(high, low)], rows_ref, [near_ref])
    for link, message in zip(colour_of_links(partner_ref), (m0_ref, m1_ref, m2_ref, m3_ref)):
        message[...] = near_ref[pl.ds(link, 1), :]


def kernel_second(
    partner_ref, ids_ref, rows_ref, near_ref, sums_ref, m0_ref, m1_ref, m2_ref, m3_ref, state_ref,
    planes_ref, depths_ref, fields_ref, corners_ref,
    later_ref, weights_ref, send_ref,
    far_ref, x_ref,
):
    receive(partner_ref, (m0_ref, m1_ref, m2_ref, m3_ref), far_ref)
    sign = signs(partner_ref)
    image = sign * (near_ref[...] - far_ref[0])
    energy, rz, work = sums_ref[0:1, 0:1], sums_ref[0:1, 1:2], sums_ref[0:1, 3:4]
    alpha = rz / (2.0 * (energy + work))
    rhs, weight = state_ref[0], state_ref[1]
    residual = rhs - alpha * image
    precond = weight * residual
    later_ref[0] = image
    later_ref[1] = residual
    later_ref[2] = precond
    later_ref[3] = weight * rhs
    x_ref[...] = sign * precond
    planes = [planes_ref[i] for i in range(4)]
    depths = [depths_ref[i] for i in range(4)]
    launch(
        ids_ref, rows_ref, x_ref, planes, depths, fields_ref, corners_ref,
        [reduce_all(residual * precond), reduce_all(precond * image)], weights_ref, send_ref,
    )


def kernel_end(
    partner_ref, near_ref, sums_ref, first_ref, m0_ref, m1_ref, m2_ref, m3_ref, later_ref,
    multipliers_ref, residual_ref,
    far_ref,
):
    receive(partner_ref, (m0_ref, m1_ref, m2_ref, m3_ref), far_ref)
    sign = signs(partner_ref)
    energy, rz, work = first_ref[0:1, 0:1], first_ref[0:1, 1:2], first_ref[0:1, 3:4]
    form = 2.0 * (energy + work)
    alpha = rz / form
    energy, rz_next, cross, work = (sums_ref[0:1, i : i + 1] for i in range(4))
    beta = rz_next / rz
    form_next = 2.0 * (energy + work) + beta * (2.0 * cross + beta * form)
    alpha_next = rz_next / form_next
    image, residual, precond, direction = (later_ref[i] for i in range(4))
    image_next = sign * (near_ref[...] - far_ref[0]) + beta * image
    direction_next = precond + beta * direction
    multipliers_ref[...] = alpha * direction + alpha_next * direction_next
    residual_ref[...] = residual - alpha_next * image_next


VMEM = pl.BlockSpec(memory_space=pltpu.VMEM)
SMEM = pl.BlockSpec(memory_space=pltpu.SMEM)


def call(kernel, name, scalars, arrays, outs, scratch=(), flops=2_000_000_000):
    shapes = [jax.ShapeDtypeStruct(*o) for o in outs]
    return pl.pallas_call(
        kernel,
        name=name,
        out_shape=shapes,
        in_specs=[SMEM] * len(scalars) + [VMEM] * len(arrays),
        out_specs=[VMEM] * len(outs),
        scratch_shapes=[pltpu.VMEM(*s) for s in scratch],
        compiler_params=pltpu.CompilerParams(vmem_limit_bytes=40 * 1024 * 1024),
        cost_estimate=pl.CostEstimate(flops=flops, bytes_accessed=4_000_000, transcendentals=0),
    )(*scalars, *arrays)


def pairing(size, first):
    pairs = []
    for i in range(first, size + first, 2):
        a, b = i % size, (i + 1) % size
        pairs += [(a, b), (b, a)]
    return pairs


def exchange(messages):
    sub = ("x", "z", "core")
    near_sub = lax.ppermute(messages[0], sub, pairing(NSUB, 0))
    far_sub = lax.ppermute(messages[1], sub, pairing(NSUB, 1))
    near_col = lax.ppermute(messages[2], "y", pairing(NY, 0))
    far_col = lax.ppermute(messages[3], "y", pairing(NY, 1))
    return near_sub, far_sub, near_col, far_col


def spread(send, axes, count):
    return lax.all_to_all(send.reshape(count * 8, 128), axes, 0, 0, tiled=True).reshape(count, 8, 128)


def on_device(
    loads, mode_x, mode_y, mode_z, eigen, classes, coefficients, partner, rows, corner_id, corner_row, coarse_inverse
):
    inverse = lax.all_gather(coarse_inverse, "y", axis=0, tiled=True)
    rows = rows[0, 0]
    partner = partner[0, 0]
    ids = corner_id[0, 0]
    halo = (2, WIDTH)
    one = (1, WIDTH)
    wide = (COLOURS, WIDTH)
    planes, depths, fields, corners, near, *messages = call(
        kernel_start,
        "start",
        [partner, corner_row[0, 0], coefficients, 1.0 / jnp.sqrt(coefficients)],
        [
            loads.reshape(PLANE, DEPTH), mode_x[0, 0], mode_y[0, 0], mode_z[0, 0], eigen[0],
            classes.reshape(16, 32), rows,
        ],
        [
            ((4, PLANE, PLANE), BF16), ((4, DEPTH, DEPTH), BF16), ((2, DEPTH, PLANE), F32), ((16, PLANE), F32),
            ((2, *wide), F32), (halo, F32), (halo, F32), (halo, F32), (halo, F32),
        ],
        [(wide, F32)],
    )
    shared = [planes, depths, fields, corners]
    messages = exchange(messages)

    def total(send):
        got = spread(send, ("z", "core"), NZ * NCORE)
        (send,) = call(kernel_relay, "relay", [], [got], [((NX * NY, 8, 128), F32)], flops=1000)
        return spread(send, ("x", "y"), NX * NY)

    weights_out = ((DEPTH, PLANE), F32)
    send_out = ((NZ * NCORE, 8, 128), F32)
    scratch = [((2, *wide), F32), (wide, F32)]
    state, weights, send = call(
        kernel_first, "first", [partner, ids], [rows, near, *messages, *shared],
        [((2, *wide), F32), weights_out, send_out], scratch,
    )
    coarse_outs = [(wide, F32), ((8, 128), F32), (one, F32), (one, F32), (one, F32), (one, F32)]
    got = total(send)
    near, first_sums, *messages = call(
        kernel_coarse, "coarse", [partner, ids], [rows, got, inverse, weights, *shared], coarse_outs
    )
    messages = exchange(messages)
    later, weights, send = call(
        kernel_second, "second", [partner, ids], [rows, near, first_sums, *messages, state, *shared],
        [((4, *wide), F32), weights_out, send_out], scratch,
    )
    got = total(send)
    near, sums, *messages = call(
        kernel_coarse, "coarse", [partner, ids], [rows, got, inverse, weights, *shared], coarse_outs
    )
    messages = exchange(messages)
    multipliers, residual = call(
        kernel_end, "end", [partner], [near, sums, first_sums, *messages, later], [(wide, F32), (wide, F32)],
        scratch[:1], flops=1000,
    )
    return multipliers[None, None], residual[None, None]


def solution(mesh):
    fine = Mesh(np.asarray(mesh.devices).reshape(NX, NZ, NCORE, NY), ("x", "z", "core", "y"))
    sub = ("x", "z", "core")
    placed = (
        P(sub, "y", None, None, None),
        P(sub, "y", None, None),
        P(sub, "y", None, None),
        P(sub, "y", None, None),
        P(sub, "y", None),
        P(sub, "y", None, None, None),
        P(),
        P(sub, "y", None, None),
        P(sub, "y", None, None),
        P(sub, "y", None),
        P(sub, "y", None),
        P("y", None),
    )
    return jax.shard_map(
        on_device,
        mesh=fine,
        in_specs=placed,
        out_specs=(P(sub, "y", None, None), P(sub, "y", None, None)),
        check_vma=False,
    )
```

```python
import functools

import jax
import jax.numpy as jnp
import numpy as np
from jax import lax
from jax.experimental import pallas as pl
from jax.experimental.pallas import tpu as pltpu
from jax.sharding import Mesh, PartitionSpec as P

F32 = jnp.float32
BF16 = jnp.bfloat16
I32 = jnp.int32

NX, NZ, NCORE, NY = 4, 12, 2, 8
NSUB = NX * NZ * NCORE
PLANE = 256
DEPTH = 128
COLOURS = 4
WIDTH = 2048
CORNERS = 8
TOTAL = 768
CHUNK = 512
NT = (((1,), (1,)), ((), ()))
TN = (((0,), (0,)), ((), ()))


def iota(shape, dim):
    return lax.broadcasted_iota(I32, shape, dim)


def split(x):
    high = x.astype(BF16)
    return high, (x - high.astype(F32)).astype(BF16)


def dot(a, b, dims=None):
    if dims is None:
        return jnp.dot(a, b, preferred_element_type=F32)
    return lax.dot_general(a, b, dims, preferred_element_type=F32)


def dot_full(a, b, dims=(((1,), (0,)), ((), ()))):
    return lax.dot_general(a, b, dims, precision=lax.Precision.HIGHEST, preferred_element_type=F32)


def thirds(x):
    high = x.astype(BF16)
    rest = x - high.astype(F32)
    middle = rest.astype(BF16)
    return high, middle, (rest - middle.astype(F32)).astype(BF16)


def product(a, b):
    (ah, am, al), (bh, bm, bl) = a, b
    return dot(ah, bh) + ((dot(am, bh) + dot(ah, bm)) + ((dot(al, bh) + dot(am, bm)) + dot(ah, bl)))


def position():
    sub = (lax.axis_index("x") * NZ + lax.axis_index("z")) * NCORE + lax.axis_index("core")
    return sub, lax.axis_index("y")


def colour_of_links(partner_ref):
    sub, col = position()
    odd_sub, odd_col = lax.rem(sub, 2), lax.rem(col, 2)
    mates = (
        (lax.rem(sub + 2 * odd_sub - 1 + NSUB, NSUB), col),
        (sub, col + 1 - 2 * odd_col),
        (sub, lax.rem(col + 2 * odd_col - 1 + NY, NY)),
        (sub + 1 - 2 * odd_sub, col),
    )
    links = []
    for mate_sub, mate_col in mates:
        colour = jnp.int32(0)
        for c in range(1, COLOURS):
            hit = (partner_ref[0, c] == mate_sub) & (partner_ref[1, c] == mate_col)
            colour = jnp.where(hit, jnp.int32(c), colour)
        links.append(colour)
    return links


def signs(partner_ref):
    sub, col = position()
    me = sub * NY + col
    which = iota((COLOURS, WIDTH), 0)
    result = jnp.full((COLOURS, WIDTH), 1.0, F32)
    for c in range(COLOURS):
        value = jnp.where(me < partner_ref[0, c] * NY + partner_ref[1, c], 1.0, -1.0).astype(F32)
        result = jnp.where(which == c, value, result)
    return result


def by_class(classes, table_ref):
    result = jnp.full(classes.shape, table_ref[0], F32)
    for k in range(1, 16):
        result = jnp.where(classes == k, table_ref[k], result)
    return result


def level(count):
    return iota((count, CHUNK), 0).astype(F32).astype(BF16)


def one_hot(levels, row):
    return jnp.where(levels == row.astype(F32).astype(BF16), jnp.ones((), BF16), jnp.zeros((), BF16))


def gather(parts, rows_ref, outs):
    stacked = jnp.concatenate([p for group in parts for p in group], axis=0)
    counts = [len(group) for group in parts]
    planes = level(PLANE)

    for j in range(WIDTH // CHUNK):
        here = slice(j * CHUNK, (j + 1) * CHUNK)
        for c in range(COLOURS):
            node = rows_ref[c : c + 1, here]
            mask = iota((DEPTH, CHUNK), 0) == (node & 127)
            picked = dot(stacked, one_hot(planes, node >> 7))
            at = 0
            for out, count in zip(outs, counts):
                total = picked[at * DEPTH : (at + 1) * DEPTH]
                for extra in range(1, count):
                    total = total + picked[(at + extra) * DEPTH : (at + extra + 1) * DEPTH]
                at += count
                out[c : c + 1, here] = jnp.sum(jnp.where(mask, total, 0.0), axis=0, keepdims=True)


def scatter(values_ref, rows_ref):
    planes, depths = level(PLANE), level(DEPTH)
    total = jnp.zeros((2 * DEPTH, PLANE), F32)
    for j in range(WIDTH // CHUNK):
        here = slice(j * CHUNK, (j + 1) * CHUNK)
        for c in range(COLOURS):
            node = rows_ref[c : c + 1, here]
            mask = depths == (node & 127).astype(F32).astype(BF16)
            parts = split(values_ref[c : c + 1, here])
            left = jnp.concatenate([jnp.where(mask, part, jnp.zeros_like(part)) for part in parts], axis=0)
            total = total + dot(left, one_hot(planes, node >> 7), NT)
    return total[:DEPTH] + total[DEPTH:]


def forward(field, planes, depths):
    return product(depths[3:], thirds(product(thirds(field), planes[:3])))


def backward(spectrum, planes, depths):
    return product(depths[:3], thirds(product(thirds(spectrum), planes[3:])))


def kernel_start(
    mode_x_hbm, mode_y_hbm, mode_z_hbm, eigen_hbm, classes_hbm, loads_hbm, rows_hbm, partner_hbm, corner_hbm, coef_hbm,
    planes_ref, depths_ref, fields_ref, corners_ref, rows_ref, near_ref, m0_ref, m1_ref, m2_ref, m3_ref,
    cls_ref, mode_x_ref, mode_y_ref, mode_z_ref, eigen_ref, classes_ref, loads_ref, partner_ref, corner_ref, coef_ref,
    sems,
):
    copies = []
    for i, (source, target) in enumerate((
        (mode_x_hbm, mode_x_ref), (mode_y_hbm, mode_y_ref), (mode_z_hbm, mode_z_ref), (eigen_hbm, eigen_ref),
        (classes_hbm, classes_ref), (loads_hbm, loads_ref), (rows_hbm, rows_ref), (partner_hbm, partner_ref),
        (corner_hbm, corner_ref), (coef_hbm, coef_ref),
    )):
        copies.append(pltpu.make_async_copy(source, target, sems.at[i]))
        copies[-1].start()
    copies[0].wait()
    copies[1].wait()
    spread_x = (iota((16, PLANE), 0) == (iota((16, PLANE), 1) >> 4)).astype(F32)
    spread_y = (iota((16, PLANE), 0) == (iota((16, PLANE), 1) & 15)).astype(F32)
    wide_x = dot_full(mode_x_ref[...], spread_x)
    wide_y = dot_full(mode_y_ref[...], spread_y)
    tall_x = dot_full(mode_x_ref[...], spread_x, TN)
    tall_y = dot_full(mode_y_ref[...], spread_y, TN)
    for i in range(16):
        here = slice(16 * i, 16 * i + 16)
        for k, part in enumerate(thirds(wide_x[i : i + 1] * wide_y) + thirds(tall_x[i : i + 1] * tall_y)):
            planes_ref[k, here] = part
    copies[2].wait()
    mode_z = mode_z_ref[...]
    for k, part in enumerate(thirds(mode_z) + thirds(mode_z.T)):
        depths_ref[k] = part
    planes = [planes_ref[i] for i in range(6)]
    depths = [depths_ref[i] for i in range(6)]

    copies[3].wait()
    line = dot_full(eigen_ref[:, 0:16], spread_x) + dot_full(eigen_ref[:, 16:32], spread_y)
    diagonal = iota((DEPTH, DEPTH), 0) == iota((DEPTH, DEPTH), 1)
    column = jnp.sum(jnp.where(diagonal, eigen_ref[:, 32:160], 0.0), axis=1, keepdims=True)
    lam_inv = 1.0 / (line + column)
    fields_ref[0] = lam_inv

    copies[4].wait()
    copies[8].wait()
    copies[9].wait()
    spread_c = (iota((16, PLANE), 0) == ((iota((16, PLANE), 1) >> 6) * 4 + ((iota((16, PLANE), 1) >> 2) & 3))).astype(BF16)
    spread_d = (iota((DEPTH, 32), 1) == (iota((DEPTH, 32), 0) >> 2)).astype(BF16)
    small = classes_ref[...].astype(F32).astype(BF16)
    deep = dot(spread_d, small, NT).astype(BF16)
    node_class = dot(deep, spread_c)
    class_part = node_class.astype(BF16)
    root = 1.0 / jnp.sqrt(by_class(node_class.astype(I32), coef_ref))
    fields_ref[1] = root

    node = jnp.zeros((CORNERS, 1), I32)
    for t in range(CORNERS):
        node = jnp.where(iota((CORNERS, 1), 0) == t, corner_ref[t], node)
    hot_plane = (iota((CORNERS, PLANE), 1) == (node >> 7)).astype(F32)
    hot_depth = (iota((CORNERS, DEPTH), 1) == (node & 127)).astype(F32)
    hot_p, hot_d = hot_plane.astype(BF16), hot_depth.astype(BF16)
    corner_class = jnp.sum(dot(hot_d, class_part) * hot_plane, axis=1, keepdims=True)
    corner_root = 1.0 / jnp.sqrt(by_class(corner_class.astype(I32), coef_ref))
    corners_ref[0:8, :] = dot(hot_p, planes[0]) + (dot(hot_p, planes[1]) + dot(hot_p, planes[2]))
    corners_ref[8:16, 0:DEPTH] = (dot(hot_d, depths[0]) + (dot(hot_d, depths[1]) + dot(hot_d, depths[2]))) * corner_root
    corners_ref[8:16, DEPTH:] = jnp.zeros((8, PLANE - DEPTH), F32)

    copies[5].wait()
    copies[6].wait()
    copies[7].wait()
    weights = forward(loads_ref[...].T * root, planes, depths) * lam_inv
    high, low = split(backward(weights, planes, depths) * root)
    gather([(high, low), (class_part,)], rows_ref, [near_ref.at[0], cls_ref])
    near_ref[1] = by_class(cls_ref[...].astype(I32), coef_ref)
    for link, message in zip(colour_of_links(partner_ref), (m0_ref, m1_ref, m2_ref, m3_ref)):
        message[0:1, :] = near_ref[0, pl.ds(link, 1), :]
        message[1:2, :] = near_ref[1, pl.ds(link, 1), :]


def reduce_all(x):
    return jnp.sum(jnp.sum(x, axis=1, keepdims=True), axis=0, keepdims=True)


def launch(ids_ref, rows_ref, x_ref, planes, depths, fields_ref, corners_ref, extras, weights_ref, send_ref):
    lam_inv, root = fields_ref[0], fields_ref[1]
    modes = forward(scatter(x_ref, rows_ref) * root, planes, depths)
    weights = modes * lam_inv
    weights_ref[...] = weights
    energy = reduce_all(weights * modes)
    part = dot_full(corners_ref[0:8, :], weights, NT) * corners_ref[8:16, 0:DEPTH]
    part = jnp.sum(part, axis=1, keepdims=True)
    lane = iota((1, 128), 1)
    row = jnp.zeros((1, 128), F32)
    for t in range(CORNERS):
        row = jnp.where(lane == t, part[t : t + 1, 0:1], row)
        row = jnp.where(lane == CORNERS + t, ids_ref[t].astype(F32), row)
    for at, scalar in enumerate([energy] + extras):
        row = jnp.where(lane == 2 * CORNERS + at, scalar, row)
    send_ref[...] = jnp.broadcast_to(row, send_ref.shape)


def receive(partner_ref, messages, far_ref):
    count = messages[0].shape[0]
    for link, message in zip(colour_of_links(partner_ref), messages):
        for i in range(count):
            far_ref[i, pl.ds(link, 1), :] = message[i : i + 1, :]


def kernel_first(
    partner_ref, ids_ref, rows_ref, near_ref, m0_ref, m1_ref, m2_ref, m3_ref,
    planes_ref, depths_ref, fields_ref, corners_ref,
    state_ref, weights_ref, send_ref,
    far_ref, x_ref,
):
    receive(partner_ref, (m0_ref, m1_ref, m2_ref, m3_ref), far_ref)
    sign = signs(partner_ref)
    a, a_far = near_ref[1], far_ref[1]
    rhs = sign * (near_ref[0] - far_ref[0])
    weight = a * a_far / (a + a_far)
    precond = weight * rhs
    state_ref[0] = rhs
    state_ref[1] = weight
    x_ref[...] = sign * precond
    planes = [planes_ref[i] for i in range(6)]
    depths = [depths_ref[i] for i in range(6)]
    launch(
        ids_ref, rows_ref, x_ref, planes, depths, fields_ref, corners_ref, [reduce_all(rhs * precond)],
        weights_ref, send_ref,
    )


def kernel_relay(got_ref, send_ref):
    got = got_ref[...]
    count = got.shape[0]
    spot = iota((count, TOTAL), 1).astype(F32)
    line = jnp.zeros((count, TOTAL), F32)
    for t in range(CORNERS):
        line = line + jnp.where(spot == got[:, CORNERS + t : CORNERS + t + 1], got[:, t : t + 1], 0.0)
    line = jnp.sum(jnp.concatenate([line, got], axis=1), axis=0, keepdims=True)
    send_ref[...] = jnp.broadcast_to(line, send_ref.shape)


def kernel_coarse(
    partner_ref, ids_ref, rows_ref, got_ref, inverse_ref, weights_ref,
    planes_ref, depths_ref, fields_ref, corners_ref,
    near_ref, sums_ref, m0_ref, m1_ref, m2_ref, m3_ref,
):
    got = jnp.sum(got_ref[...], axis=0, keepdims=True)
    line = got[:, :TOTAL]
    high = line.astype(BF16).astype(F32)
    middle = (line - high).astype(BF16).astype(F32)
    low = line - high - middle
    which = iota((8, TOTAL), 0)
    left = jnp.where(which == 0, high, jnp.where(which == 1, middle, jnp.where(which == 2, low, 0.0))).astype(BF16)
    inverse_high, inverse_low = split(inverse_ref[...])
    coarse = jnp.sum(dot(left, inverse_high) + dot(left, inverse_low), axis=0, keepdims=True)
    work = reduce_all(coarse * line)
    first = 2 * CORNERS
    sums_ref[...] = jnp.where(iota((8, 128), 1) == first + 3, work, jnp.broadcast_to(got[:, TOTAL:], (8, 128)))
    ids = jnp.zeros((CORNERS, 1), I32)
    for t in range(CORNERS):
        ids = jnp.where(iota((CORNERS, 1), 0) == t, ids_ref[t], ids)
    own = jnp.sum(jnp.where(iota((CORNERS, TOTAL), 1) == ids, coarse, 0.0), axis=1, keepdims=True)
    lam_inv, root = fields_ref[0], fields_ref[1]
    lifted = dot_full(corners_ref[8:16, 0:DEPTH] * own, corners_ref[0:8, :], TN)
    weights = weights_ref[...] + lam_inv * lifted
    planes = [planes_ref[i] for i in range(6)]
    depths = [depths_ref[i] for i in range(6)]
    high, low = split(backward(weights, planes, depths) * root)
    gather([(high, low)], rows_ref, [near_ref])
    for link, message in zip(colour_of_links(partner_ref), (m0_ref, m1_ref, m2_ref, m3_ref)):
        message[...] = near_ref[pl.ds(link, 1), :]


def scalars_of(sums_ref):
    return (sums_ref[0:1, i : i + 1] for i in range(2 * CORNERS, 2 * CORNERS + 4))


def kernel_second(
    partner_ref, ids_ref, rows_ref, near_ref, sums_ref, m0_ref, m1_ref, m2_ref, m3_ref, state_ref,
    planes_ref, depths_ref, fields_ref, corners_ref,
    later_ref, weights_ref, send_ref,
    far_ref, x_ref,
):
    receive(partner_ref, (m0_ref, m1_ref, m2_ref, m3_ref), far_ref)
    sign = signs(partner_ref)
    image = sign * (near_ref[...] - far_ref[0])
    energy, rz, _, work = scalars_of(sums_ref)
    alpha = rz / (2.0 * (energy + work))
    rhs, weight = state_ref[0], state_ref[1]
    residual = rhs - alpha * image
    precond = weight * residual
    later_ref[0] = image
    later_ref[1] = residual
    later_ref[2] = precond
    later_ref[3] = weight * rhs
    x_ref[...] = sign * precond
    planes = [planes_ref[i] for i in range(6)]
    depths = [depths_ref[i] for i in range(6)]
    launch(
        ids_ref, rows_ref, x_ref, planes, depths, fields_ref, corners_ref,
        [reduce_all(residual * precond), reduce_all(precond * image)], weights_ref, send_ref,
    )


def kernel_end(
    partner_ref, near_ref, sums_ref, first_ref, m0_ref, m1_ref, m2_ref, m3_ref, later_ref,
    multipliers_ref, residual_ref,
    far_ref,
):
    receive(partner_ref, (m0_ref, m1_ref, m2_ref, m3_ref), far_ref)
    sign = signs(partner_ref)
    energy, rz, _, work = scalars_of(first_ref)
    form = 2.0 * (energy + work)
    alpha = rz / form
    energy, rz_next, cross, work = scalars_of(sums_ref)
    beta = rz_next / rz
    form_next = 2.0 * (energy + work) + beta * (2.0 * cross + beta * form)
    alpha_next = rz_next / form_next
    image, residual, precond, direction = (later_ref[i] for i in range(4))
    image_next = sign * (near_ref[...] - far_ref[0]) + beta * image
    direction_next = precond + beta * direction
    multipliers_ref[...] = alpha * direction + alpha_next * direction_next
    residual_ref[...] = residual - alpha_next * image_next


VMEM = pl.BlockSpec(memory_space=pltpu.VMEM)
SMEM = pl.BlockSpec(memory_space=pltpu.SMEM)
HBM = pl.BlockSpec(memory_space=pltpu.HBM)


def call(kernel, name, scalars, arrays, outs, scratch=(), flops=2_000_000_000, space=VMEM):
    if space is HBM:
        arrays = [pltpu.with_memory_space_constraint(a, pltpu.HBM) for a in arrays]
    return pl.pallas_call(
        kernel,
        name=name,
        out_shape=[jax.ShapeDtypeStruct(*o) for o in outs],
        in_specs=[SMEM] * len(scalars) + [space] * len(arrays),
        out_specs=[VMEM] * len(outs),
        scratch_shapes=[pltpu.VMEM(*s) if isinstance(s, tuple) else s for s in scratch],
        compiler_params=pltpu.CompilerParams(vmem_limit_bytes=40 * 1024 * 1024),
        cost_estimate=pl.CostEstimate(flops=flops, bytes_accessed=4_000_000, transcendentals=0),
    )(*scalars, *arrays)


def pairing(size, first):
    pairs = []
    for i in range(first, size + first, 2):
        a, b = i % size, (i + 1) % size
        pairs += [(a, b), (b, a)]
    return pairs


def exchange(messages):
    sub = ("x", "z", "core")
    far_sub = lax.ppermute(messages[0], sub, pairing(NSUB, 1))
    near_col = lax.ppermute(messages[1], "y", pairing(NY, 0))
    far_col = lax.ppermute(messages[2], "y", pairing(NY, 1))
    mate = lax.ppermute(messages[3], sub, pairing(NSUB, 0))
    return far_sub, near_col, far_col, mate


def on_device(
    loads, mode_x, mode_y, mode_z, eigen, classes, coefficients, partner, rows, corner_id, corner_row, coarse_inverse
):
    inverse = lax.all_gather(coarse_inverse, "y", axis=0, tiled=True)
    partner = partner[0, 0].T
    ids = corner_id[0, 0]
    halo = (2, WIDTH)
    one = (1, WIDTH)
    wide = (COLOURS, WIDTH)
    planes, depths, fields, corners, rows, near, *messages = call(
        kernel_start,
        "start",
        [],
        [
            mode_x[0, 0], mode_y[0, 0], mode_z[0, 0], eigen[0], classes.reshape(16, 32),
            loads.reshape(PLANE, DEPTH), rows[0, 0], partner, corner_row[0, 0], coefficients,
        ],
        [
            ((6, PLANE, PLANE), BF16), ((6, DEPTH, DEPTH), BF16), ((2, DEPTH, PLANE), F32), ((16, PLANE), F32),
            (wide, I32), ((2, *wide), F32), (halo, F32), (halo, F32), (halo, F32), (halo, F32),
        ],
        [
            (wide, F32), ((16, 16), F32), ((16, 16), F32), ((DEPTH, DEPTH), F32), ((1, 160), F32), ((16, 32), I32),
            ((PLANE, DEPTH), F32), pltpu.SMEM((2, COLOURS), I32), pltpu.SMEM((CORNERS,), I32), pltpu.SMEM((16,), F32),
            pltpu.SemaphoreType.DMA((10,)),
        ],
        space=HBM,
    )
    shared = [planes, depths, fields, corners]
    messages = exchange(messages)

    def total(send):
        got = lax.all_to_all(send, ("z", "core"), 0, 0, tiled=True)
        (send,) = call(kernel_relay, "relay", [], [got], [((NX * NY, TOTAL + 128), F32)], flops=1000)
        return lax.all_to_all(send, ("x", "y"), 0, 0, tiled=True)

    weights_out = ((DEPTH, PLANE), F32)
    send_out = ((NZ * NCORE, 128), F32)
    scratch = [((2, *wide), F32), (wide, F32)]
    state, weights, send = call(
        kernel_first, "first", [partner, ids], [rows, near, *messages, *shared],
        [((2, *wide), F32), weights_out, send_out], scratch,
    )
    coarse_outs = [(wide, F32), ((8, 128), F32), (one, F32), (one, F32), (one, F32), (one, F32)]
    got = total(send)
    near, first_sums, *messages = call(
        kernel_coarse, "coarse", [partner, ids], [rows, got, inverse, weights, *shared], coarse_outs
    )
    messages = exchange(messages)
    later, weights, send = call(
        kernel_second, "second", [partner, ids], [rows, near, first_sums, *messages, state, *shared],
        [((4, *wide), F32), weights_out, send_out], scratch,
    )
    got = total(send)
    near, sums, *messages = call(
        kernel_coarse, "coarse", [partner, ids], [rows, got, inverse, weights, *shared], coarse_outs
    )
    messages = exchange(messages)
    multipliers, residual = call(
        kernel_end, "end", [partner], [near, sums, first_sums, *messages, later], [(wide, F32), (wide, F32)],
        scratch[:1], flops=1000,
    )
    return multipliers[None, None], residual[None, None]


def solution(mesh):
    fine = Mesh(np.asarray(mesh.devices).reshape(NX, NZ, NCORE, NY), ("x", "z", "core", "y"))
    sub = ("x", "z", "core")
    placed = (
        P(sub, "y", None, None, None),
        P(sub, "y", None, None),
        P(sub, "y", None, None),
        P(sub, "y", None, None),
        P(sub, "y", None),
        P(sub, "y", None, None, None),
        P(),
        P(sub, "y", None, None),
        P(sub, "y", None, None),
        P(sub, "y", None),
        P(sub, "y", None),
        P("y", None),
    )
    return jax.shard_map(
        on_device,
        mesh=fine,
        in_specs=placed,
        out_specs=(P(sub, "y", None, None), P(sub, "y", None, None)),
        check_vma=False,
    )
```

```python
import functools

import jax
import jax.numpy as jnp
import numpy as np
from jax import lax
from jax.experimental import pallas as pl
from jax.experimental.pallas import tpu as pltpu
from jax.sharding import Mesh, PartitionSpec as P

F32 = jnp.float32
BF16 = jnp.bfloat16
I32 = jnp.int32

NX, NZ, NCORE, NY = 4, 12, 2, 8
NSUB = NX * NZ * NCORE
PLANE = 256
DEPTH = 128
COLOURS = 4
WIDTH = 2048
CORNERS = 8
TOTAL = 768
SHARES = 4
CHUNK = 512
NT = (((1,), (1,)), ((), ()))
TN = (((0,), (0,)), ((), ()))


def iota(shape, dim):
    return lax.broadcasted_iota(I32, shape, dim)


def split(x):
    high = x.astype(BF16)
    return high, (x - high.astype(F32)).astype(BF16)


def dot(a, b, dims=None):
    if dims is None:
        return jnp.dot(a, b, preferred_element_type=F32)
    return lax.dot_general(a, b, dims, preferred_element_type=F32)


def dot_full(a, b, dims=(((1,), (0,)), ((), ()))):
    return lax.dot_general(a, b, dims, precision=lax.Precision.HIGHEST, preferred_element_type=F32)


def thirds(x):
    high = x.astype(BF16)
    rest = x - high.astype(F32)
    middle = rest.astype(BF16)
    return high, middle, (rest - middle.astype(F32)).astype(BF16)


def product(a, b):
    (ah, am, al), (bh, bm, bl) = a, b
    return dot(ah, bh) + ((dot(am, bh) + dot(ah, bm)) + ((dot(al, bh) + dot(am, bm)) + dot(ah, bl)))


def position():
    sub = (lax.axis_index("x") * NZ + lax.axis_index("z")) * NCORE + lax.axis_index("core")
    return sub, lax.axis_index("y")


def share():
    return lax.rem(lax.axis_index("x"), 2) * NCORE + lax.axis_index("core")


def colour_of_links(partner_ref):
    sub, col = position()
    odd_sub, odd_col = lax.rem(sub, 2), lax.rem(col, 2)
    mates = (
        (lax.rem(sub + 2 * odd_sub - 1 + NSUB, NSUB), col),
        (sub, col + 1 - 2 * odd_col),
        (sub, lax.rem(col + 2 * odd_col - 1 + NY, NY)),
        (sub + 1 - 2 * odd_sub, col),
    )
    links = []
    for mate_sub, mate_col in mates:
        colour = jnp.int32(0)
        for c in range(1, COLOURS):
            hit = (partner_ref[0, c] == mate_sub) & (partner_ref[1, c] == mate_col)
            colour = jnp.where(hit, jnp.int32(c), colour)
        links.append(colour)
    return links


def signs(partner_ref):
    sub, col = position()
    me = sub * NY + col
    which = iota((COLOURS, WIDTH), 0)
    result = jnp.full((COLOURS, WIDTH), 1.0, F32)
    for c in range(COLOURS):
        value = jnp.where(me < partner_ref[0, c] * NY + partner_ref[1, c], 1.0, -1.0).astype(F32)
        result = jnp.where(which == c, value, result)
    return result


def by_class(classes, table_ref):
    result = jnp.full(classes.shape, table_ref[0], F32)
    for k in range(1, 16):
        result = jnp.where(classes == k, table_ref[k], result)
    return result


def level(count):
    return iota((count, CHUNK), 0).astype(F32).astype(BF16)


def one_hot(levels, row):
    return jnp.where(levels == row.astype(F32).astype(BF16), jnp.ones((), BF16), jnp.zeros((), BF16))


def gather(parts, rows_ref, outs):
    stacked = jnp.concatenate([p for group in parts for p in group], axis=0)
    counts = [len(group) for group in parts]
    planes = level(PLANE)

    for j in range(WIDTH // CHUNK):
        here = slice(j * CHUNK, (j + 1) * CHUNK)
        for c in range(COLOURS):
            node = rows_ref[c : c + 1, here]
            mask = iota((DEPTH, CHUNK), 0) == (node & 127)
            picked = dot(stacked, one_hot(planes, node >> 7))
            at = 0
            for out, count in zip(outs, counts):
                total = picked[at * DEPTH : (at + 1) * DEPTH]
                for extra in range(1, count):
                    total = total + picked[(at + extra) * DEPTH : (at + extra + 1) * DEPTH]
                at += count
                out[c : c + 1, here] = jnp.sum(jnp.where(mask, total, 0.0), axis=0, keepdims=True)


def scatter(values_ref, rows_ref):
    planes, depths = level(PLANE), level(DEPTH)
    total = jnp.zeros((2 * DEPTH, PLANE), F32)
    for j in range(WIDTH // CHUNK):
        here = slice(j * CHUNK, (j + 1) * CHUNK)
        for c in range(COLOURS):
            node = rows_ref[c : c + 1, here]
            mask = depths == (node & 127).astype(F32).astype(BF16)
            parts = split(values_ref[c : c + 1, here])
            left = jnp.concatenate([jnp.where(mask, part, jnp.zeros_like(part)) for part in parts], axis=0)
            total = total + dot(left, one_hot(planes, node >> 7), NT)
    return total[:DEPTH] + total[DEPTH:]


def forward(field, planes, depths):
    return product(depths[3:], thirds(product(thirds(field), planes[:3])))


def backward(spectrum, planes, depths):
    return product(depths[:3], thirds(product(thirds(spectrum), planes[3:])))


def kernel_start(
    mode_x_hbm, mode_y_hbm, mode_z_hbm, eigen_hbm, classes_hbm, loads_hbm, rows_hbm, partner_hbm, corner_hbm, coef_hbm,
    planes_ref, depths_ref, fields_ref, corners_ref, rows_ref, near_ref, m0_ref, m1_ref, m2_ref, m3_ref,
    cls_ref, mode_x_ref, mode_y_ref, mode_z_ref, eigen_ref, classes_ref, loads_ref, partner_ref, corner_ref, coef_ref,
    sems,
):
    copies = []
    for i, (source, target) in enumerate((
        (mode_x_hbm, mode_x_ref), (mode_y_hbm, mode_y_ref), (mode_z_hbm, mode_z_ref), (eigen_hbm, eigen_ref),
        (classes_hbm, classes_ref), (loads_hbm, loads_ref), (rows_hbm, rows_ref), (partner_hbm, partner_ref),
        (corner_hbm, corner_ref), (coef_hbm, coef_ref),
    )):
        copies.append(pltpu.make_async_copy(source, target, sems.at[i]))
        copies[-1].start()
    copies[0].wait()
    copies[1].wait()
    spread_x = (iota((16, PLANE), 0) == (iota((16, PLANE), 1) >> 4)).astype(F32)
    spread_y = (iota((16, PLANE), 0) == (iota((16, PLANE), 1) & 15)).astype(F32)
    wide_x = dot_full(mode_x_ref[...], spread_x)
    wide_y = dot_full(mode_y_ref[...], spread_y)
    tall_x = dot_full(mode_x_ref[...], spread_x, TN)
    tall_y = dot_full(mode_y_ref[...], spread_y, TN)
    for i in range(16):
        here = slice(16 * i, 16 * i + 16)
        for k, part in enumerate(thirds(wide_x[i : i + 1] * wide_y) + thirds(tall_x[i : i + 1] * tall_y)):
            planes_ref[k, here] = part
    copies[2].wait()
    mode_z = mode_z_ref[...]
    for k, part in enumerate(thirds(mode_z) + thirds(mode_z.T)):
        depths_ref[k] = part
    planes = [planes_ref[i] for i in range(6)]
    depths = [depths_ref[i] for i in range(6)]

    copies[3].wait()
    line = dot_full(eigen_ref[:, 0:16], spread_x) + dot_full(eigen_ref[:, 16:32], spread_y)
    diagonal = iota((DEPTH, DEPTH), 0) == iota((DEPTH, DEPTH), 1)
    column = jnp.sum(jnp.where(diagonal, eigen_ref[:, 32:160], 0.0), axis=1, keepdims=True)
    lam_inv = 1.0 / (line + column)
    fields_ref[0] = lam_inv

    copies[4].wait()
    copies[8].wait()
    copies[9].wait()
    spread_c = (iota((16, PLANE), 0) == ((iota((16, PLANE), 1) >> 6) * 4 + ((iota((16, PLANE), 1) >> 2) & 3))).astype(BF16)
    spread_d = (iota((DEPTH, 32), 1) == (iota((DEPTH, 32), 0) >> 2)).astype(BF16)
    small = classes_ref[...].astype(F32).astype(BF16)
    deep = dot(spread_d, small, NT).astype(BF16)
    node_class = dot(deep, spread_c)
    class_part = node_class.astype(BF16)
    root = 1.0 / jnp.sqrt(by_class(node_class.astype(I32), coef_ref))
    fields_ref[1] = root

    node = jnp.zeros((CORNERS, 1), I32)
    for t in range(CORNERS):
        node = jnp.where(iota((CORNERS, 1), 0) == t, corner_ref[t], node)
    hot_plane = (iota((CORNERS, PLANE), 1) == (node >> 7)).astype(F32)
    hot_depth = (iota((CORNERS, DEPTH), 1) == (node & 127)).astype(F32)
    hot_p, hot_d = hot_plane.astype(BF16), hot_depth.astype(BF16)
    corner_class = jnp.sum(dot(hot_d, class_part) * hot_plane, axis=1, keepdims=True)
    corner_root = 1.0 / jnp.sqrt(by_class(corner_class.astype(I32), coef_ref))
    corners_ref[0:8, :] = dot(hot_p, planes[0]) + (dot(hot_p, planes[1]) + dot(hot_p, planes[2]))
    corners_ref[8:16, 0:DEPTH] = (dot(hot_d, depths[0]) + (dot(hot_d, depths[1]) + dot(hot_d, depths[2]))) * corner_root
    corners_ref[8:16, DEPTH:] = jnp.zeros((8, PLANE - DEPTH), F32)

    copies[5].wait()
    copies[6].wait()
    copies[7].wait()
    weights = forward(loads_ref[...].T * root, planes, depths) * lam_inv
    high, low = split(backward(weights, planes, depths) * root)
    gather([(high, low), (class_part,)], rows_ref, [near_ref.at[0], cls_ref])
    near_ref[1] = by_class(cls_ref[...].astype(I32), coef_ref)
    for link, message in zip(colour_of_links(partner_ref), (m0_ref, m1_ref, m2_ref, m3_ref)):
        message[0:1, :] = near_ref[0, pl.ds(link, 1), :]
        message[1:2, :] = near_ref[1, pl.ds(link, 1), :]


def reduce_all(x):
    return jnp.sum(jnp.sum(x, axis=1, keepdims=True), axis=0, keepdims=True)


def launch(ids_ref, rows_ref, x_ref, planes, depths, fields_ref, corners_ref, extras, weights_ref, send_ref):
    lam_inv, root = fields_ref[0], fields_ref[1]
    modes = forward(scatter(x_ref, rows_ref) * root, planes, depths)
    weights = modes * lam_inv
    weights_ref[...] = weights
    energy = reduce_all(weights * modes)
    part = dot_full(corners_ref[0:8, :], weights, NT) * corners_ref[8:16, 0:DEPTH]
    part = jnp.sum(part, axis=1, keepdims=True)
    lane = iota((1, 128), 1)
    row = jnp.zeros((1, 128), F32)
    for t in range(CORNERS):
        row = jnp.where(lane == t, part[t : t + 1, 0:1], row)
        row = jnp.where(lane == CORNERS + t, ids_ref[t].astype(F32), row)
    for at, scalar in enumerate([energy] + extras):
        row = jnp.where(lane == 2 * CORNERS + at, scalar, row)
    send_ref[...] = jnp.broadcast_to(row, send_ref.shape)


def receive(partner_ref, messages, far_ref):
    count = messages[0].shape[0]
    for link, message in zip(colour_of_links(partner_ref), messages):
        for i in range(count):
            far_ref[i, pl.ds(link, 1), :] = message[i : i + 1, :]


def kernel_first(
    partner_ref, ids_ref, rows_ref, near_ref, m0_ref, m1_ref, m2_ref, m3_ref,
    planes_ref, depths_ref, fields_ref, corners_ref,
    state_ref, weights_ref, send_ref,
    far_ref, x_ref,
):
    receive(partner_ref, (m0_ref, m1_ref, m2_ref, m3_ref), far_ref)
    sign = signs(partner_ref)
    a, a_far = near_ref[1], far_ref[1]
    rhs = sign * (near_ref[0] - far_ref[0])
    weight = a * a_far / (a + a_far)
    precond = weight * rhs
    state_ref[0] = rhs
    state_ref[1] = weight
    x_ref[...] = sign * precond
    planes = [planes_ref[i] for i in range(6)]
    depths = [depths_ref[i] for i in range(6)]
    launch(
        ids_ref, rows_ref, x_ref, planes, depths, fields_ref, corners_ref, [reduce_all(rhs * precond)],
        weights_ref, send_ref,
    )


def kernel_relay(got_ref, send_ref):
    got = got_ref[...]
    count = got.shape[0]
    spot = iota((count, TOTAL), 1).astype(F32)
    line = jnp.zeros((count, TOTAL), F32)
    for t in range(CORNERS):
        line = line + jnp.where(spot == got[:, CORNERS + t : CORNERS + t + 1], got[:, t : t + 1], 0.0)
    line = jnp.sum(jnp.concatenate([line, got], axis=1), axis=0, keepdims=True)
    send_ref[...] = jnp.broadcast_to(line, send_ref.shape)


def kernel_coarse(
    partner_ref, ids_ref, rows_ref, got_ref, own_ref, side_ref, mate_ref, weights_ref,
    planes_ref, depths_ref, fields_ref, corners_ref,
    near_ref, sums_ref, m0_ref, m1_ref, m2_ref, m3_ref,
):
    got = jnp.sum(got_ref[...], axis=0, keepdims=True)
    line = got[:, :TOTAL]
    high = line.astype(BF16).astype(F32)
    middle = (line - high).astype(BF16).astype(F32)
    low = line - high - middle
    which = iota((8, TOTAL), 0)
    left = jnp.where(which == 0, high, jnp.where(which == 1, middle, jnp.where(which == 2, low, 0.0)))
    coarse = jnp.zeros((8, TOTAL), F32)
    part = TOTAL // NY // SHARES
    lefts = [
        jnp.concatenate([left[:, (SHARES * i + q) * part : (SHARES * i + q + 1) * part] for i in range(NY)], axis=1)
        for q in range(SHARES)
    ]
    mine = share()
    half = NY * part
    blocks = (own_ref[...], side_ref[...], mate_ref[0:half, :], mate_ref[half:, :])
    for flip, block in zip((0, 2, 1, 3), blocks):
        chosen = lefts[flip]
        for q in range(1, SHARES):
            chosen = jnp.where(mine == q, lefts[q ^ flip], chosen)
        chosen = chosen.astype(BF16)
        block_high, block_low = split(block)
        coarse = coarse + (dot(chosen, block_high) + dot(chosen, block_low))
    coarse = jnp.sum(coarse, axis=0, keepdims=True)
    work = reduce_all(coarse * line)
    first = 2 * CORNERS
    sums_ref[...] = jnp.where(iota((8, 128), 1) == first + 3, work, jnp.broadcast_to(got[:, TOTAL:], (8, 128)))
    ids = jnp.zeros((CORNERS, 1), I32)
    for t in range(CORNERS):
        ids = jnp.where(iota((CORNERS, 1), 0) == t, ids_ref[t], ids)
    at_ids = jnp.sum(jnp.where(iota((CORNERS, TOTAL), 1) == ids, coarse, 0.0), axis=1, keepdims=True)
    lam_inv, root = fields_ref[0], fields_ref[1]
    lifted = dot_full(corners_ref[8:16, 0:DEPTH] * at_ids, corners_ref[0:8, :], TN)
    weights = weights_ref[...] + lam_inv * lifted
    planes = [planes_ref[i] for i in range(6)]
    depths = [depths_ref[i] for i in range(6)]
    high, low = split(backward(weights, planes, depths) * root)
    gather([(high, low)], rows_ref, [near_ref])
    for link, message in zip(colour_of_links(partner_ref), (m0_ref, m1_ref, m2_ref, m3_ref)):
        message[...] = near_ref[pl.ds(link, 1), :]


def scalars_of(sums_ref):
    return (sums_ref[0:1, i : i + 1] for i in range(2 * CORNERS, 2 * CORNERS + 4))


def kernel_second(
    partner_ref, ids_ref, rows_ref, near_ref, sums_ref, m0_ref, m1_ref, m2_ref, m3_ref, state_ref,
    planes_ref, depths_ref, fields_ref, corners_ref,
    later_ref, weights_ref, send_ref,
    far_ref, x_ref,
):
    receive(partner_ref, (m0_ref, m1_ref, m2_ref, m3_ref), far_ref)
    sign = signs(partner_ref)
    image = sign * (near_ref[...] - far_ref[0])
    energy, rz, _, work = scalars_of(sums_ref)
    alpha = rz / (2.0 * (energy + work))
    rhs, weight = state_ref[0], state_ref[1]
    residual = rhs - alpha * image
    precond = weight * residual
    later_ref[0] = image
    later_ref[1] = residual
    later_ref[2] = precond
    later_ref[3] = weight * rhs
    x_ref[...] = sign * precond
    planes = [planes_ref[i] for i in range(6)]
    depths = [depths_ref[i] for i in range(6)]
    launch(
        ids_ref, rows_ref, x_ref, planes, depths, fields_ref, corners_ref,
        [reduce_all(residual * precond), reduce_all(precond * image)], weights_ref, send_ref,
    )


def kernel_end(
    partner_ref, near_ref, sums_ref, first_ref, m0_ref, m1_ref, m2_ref, m3_ref, later_ref,
    multipliers_ref, residual_ref,
    far_ref,
):
    receive(partner_ref, (m0_ref, m1_ref, m2_ref, m3_ref), far_ref)
    sign = signs(partner_ref)
    energy, rz, _, work = scalars_of(first_ref)
    form = 2.0 * (energy + work)
    alpha = rz / form
    energy, rz_next, cross, work = scalars_of(sums_ref)
    beta = rz_next / rz
    form_next = 2.0 * (energy + work) + beta * (2.0 * cross + beta * form)
    alpha_next = rz_next / form_next
    image, residual, precond, direction = (later_ref[i] for i in range(4))
    image_next = sign * (near_ref[...] - far_ref[0]) + beta * image
    direction_next = precond + beta * direction
    multipliers_ref[...] = alpha * direction + alpha_next * direction_next
    residual_ref[...] = residual - alpha_next * image_next


VMEM = pl.BlockSpec(memory_space=pltpu.VMEM)
SMEM = pl.BlockSpec(memory_space=pltpu.SMEM)
HBM = pl.BlockSpec(memory_space=pltpu.HBM)


def call(kernel, name, scalars, arrays, outs, scratch=(), flops=2_000_000_000, space=VMEM):
    if space is HBM:
        arrays = [pltpu.with_memory_space_constraint(a, pltpu.HBM) for a in arrays]
    return pl.pallas_call(
        kernel,
        name=name,
        out_shape=[jax.ShapeDtypeStruct(*o) for o in outs],
        in_specs=[SMEM] * len(scalars) + [space] * len(arrays),
        out_specs=[VMEM] * len(outs),
        scratch_shapes=[pltpu.VMEM(*s) if isinstance(s, tuple) else s for s in scratch],
        compiler_params=pltpu.CompilerParams(vmem_limit_bytes=40 * 1024 * 1024),
        cost_estimate=pl.CostEstimate(flops=flops, bytes_accessed=4_000_000, transcendentals=0),
    )(*scalars, *arrays)


def pairing(size, first):
    pairs = []
    for i in range(first, size + first, 2):
        a, b = i % size, (i + 1) % size
        pairs += [(a, b), (b, a)]
    return pairs


def exchange(messages):
    sub = ("x", "z", "core")
    far_sub = lax.ppermute(messages[0], sub, pairing(NSUB, 1))
    near_col = lax.ppermute(messages[1], "y", pairing(NY, 0))
    far_col = lax.ppermute(messages[2], "y", pairing(NY, 1))
    mate = lax.ppermute(messages[3], sub, pairing(NSUB, 0))
    return far_sub, near_col, far_col, mate


def on_device(
    loads, mode_x, mode_y, mode_z, eigen, classes, coefficients, partner, rows, corner_id, corner_row, coarse_inverse
):
    part = coarse_inverse.shape[0] // SHARES
    quarter = lax.dynamic_slice(coarse_inverse, (share() * part, 0), (part, TOTAL))
    quarter = jnp.broadcast_to(quarter[None], (NY, part, TOTAL)).reshape(NY * part, TOTAL)
    own = lax.all_to_all(quarter, "y", 0, 0, tiled=True)
    partner = partner[0, 0].T
    ids = corner_id[0, 0]
    halo = (2, WIDTH)
    one = (1, WIDTH)
    wide = (COLOURS, WIDTH)
    planes, depths, fields, corners, rows, near, *messages = call(
        kernel_start,
        "start",
        [],
        [
            mode_x[0, 0], mode_y[0, 0], mode_z[0, 0], eigen[0], classes.reshape(16, 32),
            loads.reshape(PLANE, DEPTH), rows[0, 0], partner, corner_row[0, 0], coefficients,
        ],
        [
            ((6, PLANE, PLANE), BF16), ((6, DEPTH, DEPTH), BF16), ((2, DEPTH, PLANE), F32), ((16, PLANE), F32),
            (wide, I32), ((2, *wide), F32), (halo, F32), (halo, F32), (halo, F32), (halo, F32),
        ],
        [
            (wide, F32), ((16, 16), F32), ((16, 16), F32), ((DEPTH, DEPTH), F32), ((1, 160), F32), ((16, 32), I32),
            ((PLANE, DEPTH), F32), pltpu.SMEM((2, COLOURS), I32), pltpu.SMEM((CORNERS,), I32), pltpu.SMEM((16,), F32),
            pltpu.SemaphoreType.DMA((10,)),
        ],
        space=HBM,
    )
    shared = [planes, depths, fields, corners]
    messages = exchange(messages)
    messages, own = lax.optimization_barrier((messages, own))
    side = lax.ppermute(own, "x", pairing(NX, 0))

    def total(send, held):
        got = lax.all_to_all(send, ("z", "core"), 0, 0, tiled=True)
        got, held = lax.optimization_barrier((got, held))
        (send,) = call(kernel_relay, "relay", [], [got], [((NX * NY, TOTAL + 128), F32)], flops=1000)
        return lax.all_to_all(send, ("x", "y"), 0, 0, tiled=True), held

    weights_out = ((DEPTH, PLANE), F32)
    send_out = ((NZ * NCORE, 128), F32)
    scratch = [((2, *wide), F32), (wide, F32)]
    state, weights, send = call(
        kernel_first, "first", [partner, ids], [rows, near, *messages, *shared],
        [((2, *wide), F32), weights_out, send_out], scratch,
    )
    coarse_outs = [(wide, F32), ((8, 128), F32), (one, F32), (one, F32), (one, F32), (one, F32)]
    got, (own, side) = total(send, (own, side))
    mate = lax.ppermute(jnp.concatenate([own, side], axis=0), ("x", "z", "core"), pairing(NSUB, 0))
    near, first_sums, *messages = call(
        kernel_coarse, "coarse", [partner, ids], [rows, got, own, side, mate, weights, *shared], coarse_outs
    )
    messages = exchange(messages)
    later, weights, send = call(
        kernel_second, "second", [partner, ids], [rows, near, first_sums, *messages, state, *shared],
        [((4, *wide), F32), weights_out, send_out], scratch,
    )
    got, _ = total(send, ())
    near, sums, *messages = call(
        kernel_coarse, "coarse", [partner, ids], [rows, got, own, side, mate, weights, *shared], coarse_outs
    )
    messages = exchange(messages)
    multipliers, residual = call(
        kernel_end, "end", [partner], [near, sums, first_sums, *messages, later], [(wide, F32), (wide, F32)],
        scratch[:1], flops=1000,
    )
    return multipliers[None, None], residual[None, None]


def solution(mesh):
    fine = Mesh(np.asarray(mesh.devices).reshape(NX, NZ, NCORE, NY), ("x", "z", "core", "y"))
    sub = ("x", "z", "core")
    placed = (
        P(sub, "y", None, None, None),
        P(sub, "y", None, None),
        P(sub, "y", None, None),
        P(sub, "y", None, None),
        P(sub, "y", None),
        P(sub, "y", None, None, None),
        P(),
        P(sub, "y", None, None),
        P(sub, "y", None, None),
        P(sub, "y", None),
        P(sub, "y", None),
        P("y", None),
    )
    return jax.shard_map(
        on_device,
        mesh=fine,
        in_specs=placed,
        out_specs=(P(sub, "y", None, None), P(sub, "y", None, None)),
        check_vma=False,
    )
```

```python
import functools

import jax
import jax.numpy as jnp
import numpy as np
from jax import lax
from jax.experimental import pallas as pl
from jax.experimental.pallas import tpu as pltpu
from jax.sharding import Mesh, PartitionSpec as P

F32 = jnp.float32
BF16 = jnp.bfloat16
I32 = jnp.int32

NX, NZ, NCORE, NY = 4, 12, 2, 8
NSUB = NX * NZ * NCORE
PLANE = 256
DEPTH = 128
COLOURS = 4
WIDTH = 2048
CORNERS = 8
TOTAL = 768
SHARES = 4
CHUNK = 512
NT = (((1,), (1,)), ((), ()))
TN = (((0,), (0,)), ((), ()))


def iota(shape, dim):
    return lax.broadcasted_iota(I32, shape, dim)


def split(x):
    high = x.astype(BF16)
    return high, (x - high.astype(F32)).astype(BF16)


def dot(a, b, dims=None):
    if dims is None:
        return jnp.dot(a, b, preferred_element_type=F32)
    return lax.dot_general(a, b, dims, preferred_element_type=F32)


def dot_full(a, b, dims=(((1,), (0,)), ((), ()))):
    return lax.dot_general(a, b, dims, precision=lax.Precision.HIGHEST, preferred_element_type=F32)


def thirds(x):
    high = x.astype(BF16)
    rest = x - high.astype(F32)
    middle = rest.astype(BF16)
    return high, middle, (rest - middle.astype(F32)).astype(BF16)


def product(a, b):
    (ah, am, al), (bh, bm, bl) = a, b
    return dot(ah, bh) + ((dot(am, bh) + dot(ah, bm)) + ((dot(al, bh) + dot(am, bm)) + dot(ah, bl)))


def position():
    sub = (lax.axis_index("x") * NZ + lax.axis_index("z")) * NCORE + lax.axis_index("core")
    return sub, lax.axis_index("y")


def share():
    return lax.rem(lax.axis_index("x"), 2) * NCORE + lax.axis_index("core")


def colour_of_links(partner_ref):
    sub, col = position()
    odd_sub, odd_col = lax.rem(sub, 2), lax.rem(col, 2)
    mates = (
        (lax.rem(sub + 2 * odd_sub - 1 + NSUB, NSUB), col),
        (sub, col + 1 - 2 * odd_col),
        (sub, lax.rem(col + 2 * odd_col - 1 + NY, NY)),
        (sub + 1 - 2 * odd_sub, col),
    )
    links = []
    for mate_sub, mate_col in mates:
        colour = jnp.int32(0)
        for c in range(1, COLOURS):
            hit = (partner_ref[0, c] == mate_sub) & (partner_ref[1, c] == mate_col)
            colour = jnp.where(hit, jnp.int32(c), colour)
        links.append(colour)
    return links


def signs(partner_ref):
    sub, col = position()
    me = sub * NY + col
    which = iota((COLOURS, WIDTH), 0)
    result = jnp.full((COLOURS, WIDTH), 1.0, F32)
    for c in range(COLOURS):
        value = jnp.where(me < partner_ref[0, c] * NY + partner_ref[1, c], 1.0, -1.0).astype(F32)
        result = jnp.where(which == c, value, result)
    return result


def by_class(classes, table_ref):
    result = jnp.full(classes.shape, table_ref[0], F32)
    for k in range(1, 16):
        result = jnp.where(classes == k, table_ref[k], result)
    return result


def level(count):
    return iota((count, CHUNK), 0).astype(F32).astype(BF16)


def one_hot(levels, row):
    return jnp.where(levels == row.astype(F32).astype(BF16), jnp.ones((), BF16), jnp.zeros((), BF16))


def gather(parts, rows_ref, outs):
    stacked = jnp.concatenate([p for group in parts for p in group], axis=0)
    counts = [len(group) for group in parts]
    planes = level(PLANE)

    for j in range(WIDTH // CHUNK):
        here = slice(j * CHUNK, (j + 1) * CHUNK)
        for c in range(COLOURS):
            node = rows_ref[c : c + 1, here]
            mask = iota((DEPTH, CHUNK), 0) == (node & 127)
            picked = dot(stacked, one_hot(planes, node >> 7))
            at = 0
            for out, count in zip(outs, counts):
                total = picked[at * DEPTH : (at + 1) * DEPTH]
                for extra in range(1, count):
                    total = total + picked[(at + extra) * DEPTH : (at + extra + 1) * DEPTH]
                at += count
                out[c : c + 1, here] = jnp.sum(jnp.where(mask, total, 0.0), axis=0, keepdims=True)


def scatter(values_ref, rows_ref):
    planes, depths = level(PLANE), level(DEPTH)
    total = jnp.zeros((2 * DEPTH, PLANE), F32)
    for j in range(WIDTH // CHUNK):
        here = slice(j * CHUNK, (j + 1) * CHUNK)
        for c in range(COLOURS):
            node = rows_ref[c : c + 1, here]
            mask = depths == (node & 127).astype(F32).astype(BF16)
            parts = split(values_ref[c : c + 1, here])
            left = jnp.concatenate([jnp.where(mask, part, jnp.zeros_like(part)) for part in parts], axis=0)
            total = total + dot(left, one_hot(planes, node >> 7), NT)
    return total[:DEPTH] + total[DEPTH:]


def forward(field, planes, depths):
    return product(depths[3:], thirds(product(thirds(field), planes[:3])))


def backward(spectrum, planes, depths):
    return product(depths[:3], thirds(product(thirds(spectrum), planes[3:])))


def kernel_start(
    mode_x_hbm, mode_y_hbm, mode_z_hbm, eigen_hbm, classes_hbm, loads_hbm, rows_hbm, partner_hbm, corner_hbm, coef_hbm,
    planes_ref, depths_ref, fields_ref, corners_ref, rows_ref, near_ref, m0_ref, m1_ref, m2_ref, m3_ref,
    cls_ref, mode_x_ref, mode_y_ref, mode_z_ref, eigen_ref, classes_ref, loads_ref, partner_ref, corner_ref, coef_ref,
    sems,
):
    copies = []
    for i, (source, target) in enumerate((
        (mode_x_hbm, mode_x_ref), (mode_y_hbm, mode_y_ref), (mode_z_hbm, mode_z_ref), (eigen_hbm, eigen_ref),
        (classes_hbm, classes_ref), (loads_hbm, loads_ref), (rows_hbm, rows_ref), (partner_hbm, partner_ref),
        (corner_hbm, corner_ref), (coef_hbm, coef_ref),
    )):
        copies.append(pltpu.make_async_copy(source, target, sems.at[i]))
        copies[-1].start()
    for copy in copies:
        copy.wait()
    spread_x = (iota((16, PLANE), 0) == (iota((16, PLANE), 1) >> 4)).astype(F32)
    spread_y = (iota((16, PLANE), 0) == (iota((16, PLANE), 1) & 15)).astype(F32)
    wide_x = dot_full(mode_x_ref[...], spread_x)
    wide_y = dot_full(mode_y_ref[...], spread_y)
    tall_x = dot_full(mode_x_ref[...], spread_x, TN)
    tall_y = dot_full(mode_y_ref[...], spread_y, TN)
    for i in range(16):
        here = slice(16 * i, 16 * i + 16)
        for k, part in enumerate(thirds(wide_x[i : i + 1] * wide_y) + thirds(tall_x[i : i + 1] * tall_y)):
            planes_ref[k, here] = part
    mode_z = mode_z_ref[...]
    for k, part in enumerate(thirds(mode_z) + thirds(mode_z.T)):
        depths_ref[k] = part
    planes = [planes_ref[i] for i in range(6)]
    depths = [depths_ref[i] for i in range(6)]

    line = dot_full(eigen_ref[:, 0:16], spread_x) + dot_full(eigen_ref[:, 16:32], spread_y)
    diagonal = iota((DEPTH, DEPTH), 0) == iota((DEPTH, DEPTH), 1)
    column = jnp.sum(jnp.where(diagonal, eigen_ref[:, 32:160], 0.0), axis=1, keepdims=True)
    lam_inv = 1.0 / (line + column)
    fields_ref[0] = lam_inv

    spread_c = (iota((16, PLANE), 0) == ((iota((16, PLANE), 1) >> 6) * 4 + ((iota((16, PLANE), 1) >> 2) & 3))).astype(BF16)
    spread_d = (iota((DEPTH, 32), 1) == (iota((DEPTH, 32), 0) >> 2)).astype(BF16)
    small = classes_ref[...].astype(F32).astype(BF16)
    deep = dot(spread_d, small, NT).astype(BF16)
    node_class = dot(deep, spread_c)
    class_part = node_class.astype(BF16)
    root = 1.0 / jnp.sqrt(by_class(node_class.astype(I32), coef_ref))
    fields_ref[1] = root

    node = jnp.zeros((CORNERS, 1), I32)
    for t in range(CORNERS):
        node = jnp.where(iota((CORNERS, 1), 0) == t, corner_ref[t], node)
    hot_plane = (iota((CORNERS, PLANE), 1) == (node >> 7)).astype(F32)
    hot_depth = (iota((CORNERS, DEPTH), 1) == (node & 127)).astype(F32)
    hot_p, hot_d = hot_plane.astype(BF16), hot_depth.astype(BF16)
    corner_class = jnp.sum(dot(hot_d, class_part) * hot_plane, axis=1, keepdims=True)
    corner_root = 1.0 / jnp.sqrt(by_class(corner_class.astype(I32), coef_ref))
    corners_ref[0:8, :] = dot(hot_p, planes[0]) + (dot(hot_p, planes[1]) + dot(hot_p, planes[2]))
    corners_ref[8:16, 0:DEPTH] = (dot(hot_d, depths[0]) + (dot(hot_d, depths[1]) + dot(hot_d, depths[2]))) * corner_root
    corners_ref[8:16, DEPTH:] = jnp.zeros((8, PLANE - DEPTH), F32)

    weights = forward(loads_ref[...].T * root, planes, depths) * lam_inv
    high, low = split(backward(weights, planes, depths) * root)
    gather([(high, low), (class_part,)], rows_ref, [near_ref.at[0], cls_ref])
    near_ref[1] = by_class(cls_ref[...].astype(I32), coef_ref)
    for link, message in zip(colour_of_links(partner_ref), (m0_ref, m1_ref, m2_ref, m3_ref)):
        message[0:1, :] = near_ref[0, pl.ds(link, 1), :]
        message[1:2, :] = near_ref[1, pl.ds(link, 1), :]


def reduce_all(x):
    return jnp.sum(jnp.sum(x, axis=1, keepdims=True), axis=0, keepdims=True)


def launch(ids_ref, rows_ref, x_ref, planes, depths, fields_ref, corners_ref, extras, weights_ref, send_ref):
    lam_inv, root = fields_ref[0], fields_ref[1]
    modes = forward(scatter(x_ref, rows_ref) * root, planes, depths)
    weights = modes * lam_inv
    weights_ref[...] = weights
    energy = reduce_all(weights * modes)
    part = dot_full(corners_ref[0:8, :], weights, NT) * corners_ref[8:16, 0:DEPTH]
    part = jnp.sum(part, axis=1, keepdims=True)
    lane = iota((1, 128), 1)
    row = jnp.zeros((1, 128), F32)
    for t in range(CORNERS):
        row = jnp.where(lane == t, part[t : t + 1, 0:1], row)
        row = jnp.where(lane == CORNERS + t, ids_ref[t].astype(F32), row)
    for at, scalar in enumerate([energy] + extras):
        row = jnp.where(lane == 2 * CORNERS + at, scalar, row)
    send_ref[...] = jnp.broadcast_to(row, send_ref.shape)


def receive(partner_ref, messages, far_ref):
    count = messages[0].shape[0]
    for link, message in zip(colour_of_links(partner_ref), messages):
        for i in range(count):
            far_ref[i, pl.ds(link, 1), :] = message[i : i + 1, :]


def kernel_first(
    partner_ref, ids_ref, rows_ref, near_ref, m0_ref, m1_ref, m2_ref, m3_ref,
    planes_ref, depths_ref, fields_ref, corners_ref,
    state_ref, weights_ref, send_ref,
    far_ref, x_ref,
):
    receive(partner_ref, (m0_ref, m1_ref, m2_ref, m3_ref), far_ref)
    sign = signs(partner_ref)
    a, a_far = near_ref[1], far_ref[1]
    rhs = sign * (near_ref[0] - far_ref[0])
    weight = a * a_far / (a + a_far)
    precond = weight * rhs
    state_ref[0] = rhs
    state_ref[1] = weight
    x_ref[...] = sign * precond
    planes = [planes_ref[i] for i in range(6)]
    depths = [depths_ref[i] for i in range(6)]
    launch(
        ids_ref, rows_ref, x_ref, planes, depths, fields_ref, corners_ref, [reduce_all(rhs * precond)],
        weights_ref, send_ref,
    )


def kernel_relay(got_ref, send_ref):
    got = got_ref[...]
    count = got.shape[0]
    spot = iota((count, TOTAL), 1).astype(F32)
    line = jnp.zeros((count, TOTAL), F32)
    for t in range(CORNERS):
        line = line + jnp.where(spot == got[:, CORNERS + t : CORNERS + t + 1], got[:, t : t + 1], 0.0)
    line = jnp.sum(jnp.concatenate([line, got], axis=1), axis=0, keepdims=True)
    send_ref[...] = jnp.broadcast_to(line, send_ref.shape)


def kernel_coarse(
    partner_ref, ids_ref, rows_ref, got_ref, own_ref, side_ref, mate_ref, weights_ref,
    planes_ref, depths_ref, fields_ref, corners_ref,
    near_ref, sums_ref, m0_ref, m1_ref, m2_ref, m3_ref,
):
    got = jnp.sum(got_ref[...], axis=0, keepdims=True)
    line = got[:, :TOTAL]
    high = line.astype(BF16).astype(F32)
    middle = (line - high).astype(BF16).astype(F32)
    low = line - high - middle
    which = iota((8, TOTAL), 0)
    left = jnp.where(which == 0, high, jnp.where(which == 1, middle, jnp.where(which == 2, low, 0.0)))
    coarse = jnp.zeros((8, TOTAL), F32)
    part = TOTAL // NY // SHARES
    lefts = [
        jnp.concatenate([left[:, (SHARES * i + q) * part : (SHARES * i + q + 1) * part] for i in range(NY)], axis=1)
        for q in range(SHARES)
    ]
    mine = share()
    half = NY * part
    blocks = (own_ref[...], side_ref[...], mate_ref[0:half, :], mate_ref[half:, :])
    for flip, block in zip((0, 2, 1, 3), blocks):
        chosen = lefts[flip]
        for q in range(1, SHARES):
            chosen = jnp.where(mine == q, lefts[q ^ flip], chosen)
        chosen = chosen.astype(BF16)
        block_high, block_low = split(block)
        coarse = coarse + (dot(chosen, block_high) + dot(chosen, block_low))
    coarse = jnp.sum(coarse, axis=0, keepdims=True)
    work = reduce_all(coarse * line)
    first = 2 * CORNERS
    sums_ref[...] = jnp.where(iota((8, 128), 1) == first + 3, work, jnp.broadcast_to(got[:, TOTAL:], (8, 128)))
    ids = jnp.zeros((CORNERS, 1), I32)
    for t in range(CORNERS):
        ids = jnp.where(iota((CORNERS, 1), 0) == t, ids_ref[t], ids)
    at_ids = jnp.sum(jnp.where(iota((CORNERS, TOTAL), 1) == ids, coarse, 0.0), axis=1, keepdims=True)
    lam_inv, root = fields_ref[0], fields_ref[1]
    lifted = dot_full(corners_ref[8:16, 0:DEPTH] * at_ids, corners_ref[0:8, :], TN)
    weights = weights_ref[...] + lam_inv * lifted
    planes = [planes_ref[i] for i in range(6)]
    depths = [depths_ref[i] for i in range(6)]
    high, low = split(backward(weights, planes, depths) * root)
    gather([(high, low)], rows_ref, [near_ref])
    for link, message in zip(colour_of_links(partner_ref), (m0_ref, m1_ref, m2_ref, m3_ref)):
        message[...] = near_ref[pl.ds(link, 1), :]


def scalars_of(sums_ref):
    return (sums_ref[0:1, i : i + 1] for i in range(2 * CORNERS, 2 * CORNERS + 4))


def kernel_second(
    partner_ref, ids_ref, rows_ref, near_ref, sums_ref, m0_ref, m1_ref, m2_ref, m3_ref, state_ref,
    planes_ref, depths_ref, fields_ref, corners_ref,
    later_ref, weights_ref, send_ref,
    far_ref, x_ref,
):
    receive(partner_ref, (m0_ref, m1_ref, m2_ref, m3_ref), far_ref)
    sign = signs(partner_ref)
    image = sign * (near_ref[...] - far_ref[0])
    energy, rz, _, work = scalars_of(sums_ref)
    alpha = rz / (2.0 * (energy + work))
    rhs, weight = state_ref[0], state_ref[1]
    residual = rhs - alpha * image
    precond = weight * residual
    later_ref[0] = image
    later_ref[1] = residual
    later_ref[2] = precond
    later_ref[3] = weight * rhs
    x_ref[...] = sign * precond
    planes = [planes_ref[i] for i in range(6)]
    depths = [depths_ref[i] for i in range(6)]
    launch(
        ids_ref, rows_ref, x_ref, planes, depths, fields_ref, corners_ref,
        [reduce_all(residual * precond), reduce_all(precond * image)], weights_ref, send_ref,
    )


def kernel_end(
    partner_ref, near_ref, sums_ref, first_ref, m0_ref, m1_ref, m2_ref, m3_ref, later_ref,
    multipliers_ref, residual_ref,
    far_ref,
):
    receive(partner_ref, (m0_ref, m1_ref, m2_ref, m3_ref), far_ref)
    sign = signs(partner_ref)
    energy, rz, _, work = scalars_of(first_ref)
    form = 2.0 * (energy + work)
    alpha = rz / form
    energy, rz_next, cross, work = scalars_of(sums_ref)
    beta = rz_next / rz
    form_next = 2.0 * (energy + work) + beta * (2.0 * cross + beta * form)
    alpha_next = rz_next / form_next
    image, residual, precond, direction = (later_ref[i] for i in range(4))
    image_next = sign * (near_ref[...] - far_ref[0]) + beta * image
    direction_next = precond + beta * direction
    multipliers_ref[...] = alpha * direction + alpha_next * direction_next
    residual_ref[...] = residual - alpha_next * image_next


VMEM = pl.BlockSpec(memory_space=pltpu.VMEM)
SMEM = pl.BlockSpec(memory_space=pltpu.SMEM)
HBM = pl.BlockSpec(memory_space=pltpu.HBM)


def call(kernel, name, scalars, arrays, outs, scratch=(), flops=2_000_000_000, space=VMEM):
    if space is HBM:
        arrays = [pltpu.with_memory_space_constraint(a, pltpu.HBM) for a in arrays]
    return pl.pallas_call(
        kernel,
        name=name,
        out_shape=[jax.ShapeDtypeStruct(*o) for o in outs],
        in_specs=[SMEM] * len(scalars) + [space] * len(arrays),
        out_specs=[VMEM] * len(outs),
        scratch_shapes=[pltpu.VMEM(*s) if isinstance(s, tuple) else s for s in scratch],
        compiler_params=pltpu.CompilerParams(vmem_limit_bytes=40 * 1024 * 1024),
        cost_estimate=pl.CostEstimate(flops=flops, bytes_accessed=4_000_000, transcendentals=0),
    )(*scalars, *arrays)


def pairing(size, first):
    pairs = []
    for i in range(first, size + first, 2):
        a, b = i % size, (i + 1) % size
        pairs += [(a, b), (b, a)]
    return pairs


def exchange(messages):
    sub = ("x", "z", "core")
    far_sub = lax.ppermute(messages[0], sub, pairing(NSUB, 1))
    near_col = lax.ppermute(messages[1], "y", pairing(NY, 0))
    far_col = lax.ppermute(messages[2], "y", pairing(NY, 1))
    mate = lax.ppermute(messages[3], sub, pairing(NSUB, 0))
    return far_sub, near_col, far_col, mate


def on_device(
    loads, mode_x, mode_y, mode_z, eigen, classes, coefficients, partner, rows, corner_id, corner_row, coarse_inverse
):
    part = coarse_inverse.shape[0] // SHARES
    quarter = lax.dynamic_slice(coarse_inverse, (share() * part, 0), (part, TOTAL))
    quarter = jnp.broadcast_to(quarter[None], (NY, part, TOTAL)).reshape(NY * part, TOTAL)
    own = lax.all_to_all(quarter, "y", 0, 0, tiled=True)
    partner = partner[0, 0].T
    ids = corner_id[0, 0]
    halo = (2, WIDTH)
    one = (1, WIDTH)
    wide = (COLOURS, WIDTH)
    planes, depths, fields, corners, rows, near, *messages = call(
        kernel_start,
        "start",
        [],
        [
            mode_x[0, 0], mode_y[0, 0], mode_z[0, 0], eigen[0], classes.reshape(16, 32),
            loads.reshape(PLANE, DEPTH), rows[0, 0], partner, corner_row[0, 0], coefficients,
        ],
        [
            ((6, PLANE, PLANE), BF16), ((6, DEPTH, DEPTH), BF16), ((2, DEPTH, PLANE), F32), ((16, PLANE), F32),
            (wide, I32), ((2, *wide), F32), (halo, F32), (halo, F32), (halo, F32), (halo, F32),
        ],
        [
            (wide, F32), ((16, 16), F32), ((16, 16), F32), ((DEPTH, DEPTH), F32), ((1, 160), F32), ((16, 32), I32),
            ((PLANE, DEPTH), F32), pltpu.SMEM((2, COLOURS), I32), pltpu.SMEM((CORNERS,), I32), pltpu.SMEM((16,), F32),
            pltpu.SemaphoreType.DMA((10,)),
        ],
        space=HBM,
    )
    shared = [planes, depths, fields, corners]
    messages = exchange(messages)
    messages, own = lax.optimization_barrier((messages, own))
    side = lax.ppermute(own, "x", pairing(NX, 0))

    def total(send, held):
        got = lax.all_to_all(send, ("z", "core"), 0, 0, tiled=True)
        got, held = lax.optimization_barrier((got, held))
        (send,) = call(kernel_relay, "relay", [], [got], [((NX * NY, TOTAL + 128), F32)], flops=1000)
        return lax.all_to_all(send, ("x", "y"), 0, 0, tiled=True), held

    weights_out = ((DEPTH, PLANE), F32)
    send_out = ((NZ * NCORE, 128), F32)
    scratch = [((2, *wide), F32), (wide, F32)]
    state, weights, send = call(
        kernel_first, "first", [partner, ids], [rows, near, *messages, *shared],
        [((2, *wide), F32), weights_out, send_out], scratch,
    )
    coarse_outs = [(wide, F32), ((8, 128), F32), (one, F32), (one, F32), (one, F32), (one, F32)]
    got, (own, side) = total(send, (own, side))
    mate = lax.ppermute(jnp.concatenate([own, side], axis=0), ("x", "z", "core"), pairing(NSUB, 0))
    near, first_sums, *messages = call(
        kernel_coarse, "coarse", [partner, ids], [rows, got, own, side, mate, weights, *shared], coarse_outs
    )
    messages = exchange(messages)
    later, weights, send = call(
        kernel_second, "second", [partner, ids], [rows, near, first_sums, *messages, state, *shared],
        [((4, *wide), F32), weights_out, send_out], scratch,
    )
    got, _ = total(send, ())
    near, sums, *messages = call(
        kernel_coarse, "coarse", [partner, ids], [rows, got, own, side, mate, weights, *shared], coarse_outs
    )
    messages = exchange(messages)
    multipliers, residual = call(
        kernel_end, "end", [partner], [near, sums, first_sums, *messages, later], [(wide, F32), (wide, F32)],
        scratch[:1], flops=1000,
    )
    return multipliers[None, None], residual[None, None]


def solution(mesh):
    fine = Mesh(np.asarray(mesh.devices).reshape(NX, NZ, NCORE, NY), ("x", "z", "core", "y"))
    sub = ("x", "z", "core")
    placed = (
        P(sub, "y", None, None, None),
        P(sub, "y", None, None),
        P(sub, "y", None, None),
        P(sub, "y", None, None),
        P(sub, "y", None),
        P(sub, "y", None, None, None),
        P(),
        P(sub, "y", None, None),
        P(sub, "y", None, None),
        P(sub, "y", None),
        P(sub, "y", None),
        P("y", None),
    )
    return jax.shard_map(
        on_device,
        mesh=fine,
        in_specs=placed,
        out_specs=(P(sub, "y", None, None), P(sub, "y", None, None)),
        check_vma=False,
    )
```
